128 devices in a mesh: dp: 32 (over z, x, core), rep: 4 (over y).
Axes of the slice: x: 4, y: 4, z: 4, core: 2. Of those that a mesh axis runs over, the one named last changes fastest.
Arguments:
- token_inputs: bfloat16 [65536, 2048], P(('dp', 'rep')), may hold values from -12 to 12
- cotangent: bfloat16 [65536, 2048], P(('dp', 'rep')), may hold values from -24 to 24
- gate_preact: bfloat16 [65536, 768], P(('dp', 'rep')), may hold values from -6 to 6
- up_preact: bfloat16 [65536, 768], P(('dp', 'rep')), may hold values from -6 to 6
- down_weight: bfloat16 [2, 768, 2048], P(None, None, 'dp'), may hold values from -0.21875 to 0.21875
- block_expert: int32 [512], P(('dp', 'rep')), may hold values from 0 to 1
- block_count: int32 [512], P(('dp', 'rep')), may hold values from 1 to 128, as said below
Outputs:
- update: bfloat16 [2, 3, 768, 2048], P(None, None, None, 'dp')
The draws below stay inside these ranges and needn't reach their ends.
Inputs may be any that keep to these rules, and one draw needn't show every extreme that they name: `block_count`: live rows of a block, at most 128; in every draw some block is full.
All inputs are finite; a program needn't handle non-finite values.
Results may differ from the reference program's by a relative error of at most 0.02.
Values may be sent and summed in bfloat16 or wider, within the bound.
A program may use at most 128 MiB of HBM per device.

```python
import jax
import jax.numpy as jnp
from jax import lax

D = 2048
F = 768
EXPERTS = 2
BLOCK = 128
BLK = 4
ITERS = 2
ROWS = 65536
BLOCKS_ALL = 512
N_DP = 32
N_REP = 4


def draw_block_count(key, part):
    counts = jax.random.randint(key, (BLOCKS_ALL,), max(1, BLOCK // 4), BLOCK + 1, dtype=jnp.int32)
    chosen = jax.random.randint(jax.random.fold_in(key, 7), (), 0, BLOCKS_ALL, dtype=jnp.int32)
    return jnp.where(jnp.arange(BLOCKS_ALL, dtype=jnp.int32) == chosen, jnp.int32(BLOCK), counts)


def draw_token_inputs(key, part):
    column = jnp.arange(D, dtype=jnp.float32) / jnp.float32(max(D - 1, 1))
    ratio = 2.5
    base = jnp.clip(jax.random.normal(key, (ROWS, D), jnp.float32), -6.0, 6.0)
    scale = jnp.exp(jnp.log(jnp.float32(ratio)) * (column - 0.5))
    return (base * scale[None, :]).astype(jnp.bfloat16)


def plant(values, own_key, smallest, top_value):
    spot = [jax.random.randint(jax.random.fold_in(own_key, axis), (), 0, length) for axis, length in enumerate(values.shape)]
    longest = values.shape.index(max(values.shape))
    neighbour = spot[:longest] + [(spot[longest] + 1) % values.shape[longest]] + spot[longest + 1:]
    return values.at[tuple(spot)].set(smallest).at[tuple(neighbour)].set(top_value)


def spiked(values, own_key, source, target, shards_of, factor):
    def block_of(dim):
        return (jnp.arange(values.shape[dim]) // (values.shape[dim] // shards_of)).reshape((-1,) + (1,) * (values.ndim - 1 - dim))

    first = jax.random.permutation(own_key, shards_of)[block_of(target)]
    far = (block_of(target) + shards_of // 2) % shards_of
    return jnp.where((block_of(source) == first) | (block_of(source) == far), factor * values, values)


def level_of(stream_key, extent, shards, low, high):
    factor_of, own = 1.0, jax.random.fold_in(stream_key, 6)
    for position, blocks in shards:
        draws = jnp.exp(jax.random.uniform(jax.random.fold_in(own, position), (blocks,), jnp.float32, low / len(shards), high / len(shards)))
        factor_of = factor_of * jnp.repeat(draws, extent[position] // blocks).reshape([-1 if axis == position else 1 for axis in range(len(extent))])
    return factor_of


def normal_values(rng, dims, scale, most, pieces=(), kind=jnp.bfloat16):
    values = scale * jax.random.normal(rng, dims, jnp.float32)
    if pieces:
        values = values * level_of(rng, dims, pieces, -0.22, 0.18)
    return jnp.clip(values, -most, most).astype(kind)


def noise_with(key, extent, deviation, bound, pieces, heavy, held_as=jnp.bfloat16):
    drawn = deviation * jax.random.normal(key, extent, jnp.float32)
    if pieces:
        drawn = drawn * level_of(key, extent, pieces, -0.22, 0.18)
    return jnp.clip(spiked(drawn, jax.random.fold_in(key, 3), *heavy), -bound, bound).astype(held_as)


def setup_inputs(seed: int = 0) -> dict:
    key_list = jax.random.split(jax.random.key(seed), 8)
    token_inputs = draw_token_inputs(jax.random.fold_in(key_list[7], 71), 0)
    cotangent = noise_with(key_list[1], (ROWS, D), 1.0, 24.0, ((0, 128),), (0, 1, 128, 5.5))
    gate_preact = normal_values(key_list[2], (ROWS, F), 1.0, 6.0, ((0, 128),))
    up_preact = normal_values(key_list[3], (ROWS, F), 1.0, 6.0, ((0, 128),))
    down_weight = normal_values(key_list[4], (EXPERTS, F, D), F ** -0.5, 0.21875, ((2, 32),))
    block_expert = plant(jax.random.randint(key_list[5], (BLOCKS_ALL,), 0, EXPERTS), jax.random.fold_in(key_list[5], 1), 0, EXPERTS - 1).astype(jnp.int32)
    block_count = draw_block_count(jax.random.fold_in(key_list[7], 71), 0)
    return dict(token_inputs=token_inputs, cotangent=cotangent, gate_preact=gate_preact, up_preact=up_preact, down_weight=down_weight, block_expert=block_expert, block_count=block_count)


ns_first = 3.4445
ns_second = -4.775
ns_third = 2.0315
norm_eps = 1e-07

def device_partial(inputs, cotangent, gate_preact, up_preact, down_weight, experts, counts):
    blocks = counts.shape[0]
    width = inputs.shape[1]
    hidden_width = gate_preact.shape[1]
    inputs = inputs.reshape(blocks, BLOCK, width)
    cotangent = cotangent.reshape(blocks, BLOCK, width)
    gate = gate_preact.reshape(blocks, BLOCK, hidden_width).astype(jnp.float32)
    upper = up_preact.reshape(blocks, BLOCK, hidden_width).astype(jnp.float32)
    live_rows = jnp.arange(BLOCK, dtype=jnp.int32)[None, :] < counts[:, None]
    masked = jnp.where(live_rows[:, :, None], cotangent, jnp.zeros_like(cotangent))
    sigmoid_gate = jax.nn.sigmoid(gate)
    hidden = (gate * sigmoid_gate * upper).astype(jnp.bfloat16)
    chosen = jnp.take(down_weight, experts, axis=0)
    back = jnp.einsum('brd,bfd->brf', masked.astype(jnp.float32), chosen.astype(jnp.float32))
    grad_gate = (back * upper * sigmoid_gate * (1.0 + gate * (1.0 - sigmoid_gate))).astype(jnp.bfloat16)
    grad_up = (back * gate * sigmoid_gate).astype(jnp.bfloat16)
    left = jnp.stack([grad_gate, grad_up, hidden], 1).astype(jnp.float32)
    right = jnp.stack([inputs, inputs, masked], 1).astype(jnp.float32)
    per_block = jnp.einsum('bmrf,bmrd->bmfd', left, right)
    onehot = (experts[:, None] == jnp.arange(EXPERTS, dtype=jnp.int32)[None, :]).astype(jnp.float32)
    partial_value = jnp.einsum('be,bmfd->emfd', onehot, per_block, precision=lax.Precision.HIGHEST)
    return partial_value.astype(jnp.bfloat16)

def reference(token_inputs, cotangent, gate_preact, up_preact, down_weight, block_expert, block_count):
    devices_all = N_DP * N_REP
    rows_dev = BLK * BLOCK

    def add_device(total, index):
        first = (index * rows_dev).astype(jnp.int32)
        first_block = (index * BLK).astype(jnp.int32)
        partial_value = device_partial(lax.dynamic_slice_in_dim(token_inputs, first, rows_dev, 0), lax.dynamic_slice_in_dim(cotangent, first, rows_dev, 0), lax.dynamic_slice_in_dim(gate_preact, first, rows_dev, 0), lax.dynamic_slice_in_dim(up_preact, first, rows_dev, 0), down_weight, lax.dynamic_slice_in_dim(block_expert, first_block, BLK, 0), lax.dynamic_slice_in_dim(block_count, first_block, BLK, 0))
        return (total + partial_value.astype(jnp.float32), None)
    start_total = jnp.zeros((EXPERTS, 3, F, D), jnp.float32)
    grad, unused = lax.scan(add_device, start_total, jnp.arange(devices_all, dtype=jnp.int32))
    squares = lax.optimization_barrier(jnp.sum(grad * grad, axis=(2, 3)))
    current = (grad / (jnp.sqrt(squares) + norm_eps)[:, :, None, None]).astype(jnp.bfloat16)
    column_width = D // N_DP
    result = None
    for sweep in range(ITERS):
        as_float = current.astype(jnp.float32)
        split = as_float.reshape(EXPERTS, 3, F, N_DP, column_width)

        def add_columns(total, index):
            block_cols = lax.dynamic_index_in_dim(split, index, 3, False)
            term = jnp.einsum('emfd,emgd->emfg', block_cols, block_cols).astype(jnp.bfloat16)
            return (total + lax.optimization_barrier(term).astype(jnp.float32), None)
        gram, unused = lax.scan(add_columns, jnp.zeros((EXPERTS, 3, F, F), jnp.float32), jnp.arange(N_DP, dtype=jnp.int32))
        gram_half = gram.astype(jnp.bfloat16).astype(jnp.float32)
        squared = jnp.einsum('emfg,emgh->emfh', gram_half, gram_half)
        poly = (ns_second * gram + ns_third * squared).astype(jnp.bfloat16)
        newer = ns_first * as_float + jnp.einsum('emfg,emgd->emfd', poly.astype(jnp.float32), as_float)
        if sweep + 1 < ITERS:
            current = newer.astype(jnp.bfloat16)
        else:
            result = (jnp.sqrt(jnp.float32(D)) * newer).astype(jnp.bfloat16)
    return result
```

```python
import functools

import jax
import jax.numpy as jnp
from jax import lax
from jax.experimental import pallas as pl
from jax.experimental.pallas import tpu as pltpu
from jax.sharding import Mesh
from jax.sharding import PartitionSpec as P

D = 2048
F = 768
ROWS = 512
HALF = F // 2
THIRD = HALF // 2
LANES = 128
AXES = ("z", "x", "y")
ORDERS = (("z", "x", "y"), ("x", "y", "z"), ("y", "z", "x"))
MESH = pl.DeviceIdType.MESH

ns_first = 3.4445
ns_second = -4.775
ns_third = 2.0315
norm_eps = 1e-07

bf16 = jnp.bfloat16
f32 = jnp.float32


def around(axis):
    i = lax.axis_index(axis)
    return i, lax.rem(i + 1, 4), lax.rem(i + 3, 4), lax.rem(i + 2, 4)


def push(src, dst, send, recv, device):
    copy = pltpu.make_async_remote_copy(
        src_ref=src, dst_ref=dst, send_sem=send, recv_sem=recv, device_id=device, device_id_type=MESH
    )
    copy.start()
    return copy


def greet(axes, with_core):
    barrier = pltpu.get_barrier_semaphore()
    count = 0
    for axis in axes:
        i, right, left, far = around(axis)
        for other in (right, left):
            pl.semaphore_signal(barrier, inc=1, device_id={axis: other}, device_id_type=MESH)
            count += 1
    if with_core:
        c = lax.axis_index("core")
        pl.semaphore_signal(barrier, inc=1, device_id={"core": 1 - c}, device_id_type=MESH)
        count += 1
    pl.semaphore_wait(barrier, count)


class Scatter:
    def __init__(self, axis, src, first, second, near, final, send, recv, add):
        self.axis, self.src, self.first, self.second = axis, src, first, second
        self.near, self.final, self.send, self.recv, self.add = near, final, send, recv, add

    def start(self):
        i, right, left, far = around(self.axis)
        src, first, second, send, recv = self.src, self.first, self.second, self.send, self.recv
        to_right, to_left = {self.axis: right}, {self.axis: left}
        self.a1 = push(first(src.at[far]), first(self.near), send.at[0], recv.at[0], to_right)
        self.b1 = push(second(src.at[far]), second(self.near), send.at[1], recv.at[1], to_left)
        self.a2 = push(second(src.at[right]), second(self.final.at[0]), send.at[2], recv.at[2], to_right)
        self.b2 = push(first(src.at[left]), first(self.final.at[1]), send.at[3], recv.at[3], to_left)

    def middle(self):
        i, right, left, far = around(self.axis)
        src, first, second, send, recv = self.src, self.first, self.second, self.send, self.recv
        self.a1.wait_recv()
        self.add(first(src.at[right]), (first(self.near),))
        self.a3 = push(first(src.at[right]), first(self.final.at[0]), send.at[4], recv.at[4], {self.axis: right})
        self.b1.wait_recv()
        self.add(second(src.at[left]), (second(self.near),))
        self.b3 = push(second(src.at[left]), second(self.final.at[1]), send.at[5], recv.at[5], {self.axis: left})

    def finish(self):
        i, right, left, far = around(self.axis)
        for copy in (self.a2, self.b2, self.a3, self.b3):
            copy.wait_recv()
        self.add(self.src.at[i], (self.final.at[0], self.final.at[1]))

    def drain(self):
        for copy in (self.a1, self.b1, self.a2, self.b2, self.a3, self.b3):
            copy.wait_send()


class Gather:
    def __init__(self, axis, buf, first, second, send, recv):
        self.axis, self.buf, self.first, self.second = axis, buf, first, second
        self.send, self.recv = send, recv

    def start(self):
        i, right, left, far = around(self.axis)
        buf = self.buf
        self.a1 = push(buf.at[i], buf.at[i], self.send.at[0], self.recv.at[0], {self.axis: right})
        self.b1 = push(buf.at[i], buf.at[i], self.send.at[1], self.recv.at[1], {self.axis: left})

    def middle(self):
        i, right, left, far = around(self.axis)
        buf, first, second = self.buf, self.first, self.second
        self.a1.wait_recv()
        self.a2 = push(first(buf.at[left]), first(buf.at[left]), self.send.at[2], self.recv.at[2], {self.axis: right})
        self.b1.wait_recv()
        self.b2 = push(second(buf.at[right]), second(buf.at[right]), self.send.at[3], self.recv.at[3], {self.axis: left})

    def finish(self):
        self.a2.wait_recv()
        self.b2.wait_recv()

    def drain(self):
        for copy in (self.a1, self.b1, self.a2, self.b2):
            copy.wait_send()


def add_blocks(dst, others):
    lead = dst.shape[:-2]
    count = 1
    for size in lead:
        count *= size

    def one(n, carry):
        index = []
        rest = n
        for size in reversed(lead):
            index.append(lax.rem(rest, size))
            rest = lax.div(rest, size)
        index = tuple(reversed(index))
        total = dst[index].astype(f32)
        for other in others:
            total = total + other[index].astype(f32)
        dst[index] = total.astype(bf16)
        return carry

    if count == 1:
        one(0, 0)
    else:
        lax.fori_loop(0, count, one, 0)


def lead_halves(size):
    half = size // 2
    return (lambda ref: ref.at[pl.ds(0, half)]), (lambda ref: ref.at[pl.ds(half, half)])


def lane_halves(size, cut):
    return (lambda ref: ref.at[:, pl.ds(0, cut)]), (lambda ref: ref.at[:, pl.ds(cut, size - cut)])


def grad_kernel(
    masked, tokens, gate_t, up_t, row_expert, w_pad, out,
    mk, tk, gb, ub, rex, wx, wall, left_side, part,
    near0, fin0, near1, fin1, near2, fin2,
    own_sem, x_send, x_recv, w_send, w_recv, r_send, r_recv,
):
    c = lax.axis_index("core")
    other = {"core": 1 - c}
    sources = (w_pad.at[c], gate_t.at[c], up_t.at[c], row_expert, masked, tokens)
    gives = (w_pad.at[1 - c], gate_t.at[1 - c], up_t.at[1 - c], row_expert, masked, tokens)
    places = (wx, gb, ub, rex, mk, tk)
    own = []
    for n in range(6):
        copy = pltpu.make_async_copy(sources[n], places[n].at[0], own_sem.at[n])
        copy.start()
        own.append(copy)
    greet(AXES, True)
    cross = [
        push(gives[n], places[n].at[1], x_send.at[n], x_recv.at[n], other) for n in range(6)
    ]

    def ready(n):
        own[n].wait()
        cross[n].wait_recv()

    z, x = lax.axis_index("z"), lax.axis_index("x")
    first, second = lead_halves(HALF)
    four_first, four_second = lead_halves(4)
    w_near = [
        Gather("z", wall.at[0, x], first, second, w_send.at[0], w_recv.at[0]),
        Gather("x", wall.at[1, z], first, second, w_send.at[1], w_recv.at[1]),
    ]
    w_far = [
        Gather("x", wall.at[0], four_first, four_second, w_send.at[2], w_recv.at[2]),
        Gather("z", wall.at[1], four_first, four_second, w_send.at[3], w_recv.at[3]),
    ]
    ready(0)
    wall[0, x, z] = wx[0, 0] + wx[1, 0]
    wall[1, z, x] = wx[0, 1] + wx[1, 1]
    for one in w_near:
        one.start()

    rs = []
    cut0, cut1, cut2 = lead_halves(4), lead_halves(4), lead_halves(THIRD)
    for k in range(3):
        order = ORDERS[k]
        a, b = lax.axis_index(order[0]), lax.axis_index(order[1])
        rs.append(
            (
                Scatter(order[0], part.at[k], *cut0, near0.at[k], fin0.at[k], r_send.at[k, 0], r_recv.at[k, 0], add_blocks),
                Scatter(order[1], part.at[k, a], *cut1, near1.at[k], fin1.at[k], r_send.at[k, 1], r_recv.at[k, 1], add_blocks),
                Scatter(order[2], part.at[k, a, b], *cut2, near2.at[k], fin2.at[k], r_send.at[k, 2], r_recv.at[k, 2], add_blocks),
            )
        )

    for n in (1, 2, 3):
        ready(n)
    tile = 32
    for s in range(2):
        @pl.loop(0, HALF // tile)
        def hidden_rows(t, s=s):
            rows = pl.ds(pl.multiple_of(t * tile, tile), tile)
            gate = gb[s, rows, :].astype(f32)
            upper = ub[s, rows, :].astype(f32)
            hidden = gate * jax.nn.sigmoid(gate) * upper
            which = rex[s, 0:1, :]
            half = lax.div(t, THIRD // tile)
            place = pl.ds(pl.multiple_of(lax.rem(t, THIRD // tile) * tile, tile), tile)
            for e in range(2):
                kept = jnp.where(which == e, hidden, 0.0).astype(bf16)
                left_side[2, 2 * e + half, place, s * ROWS:(s + 1) * ROWS] = kept

    for one in w_near:
        one.middle()

    def products(k, right):
        lhs = left_side.at[k]

        @pl.loop(0, 4)
        def columns(iz):
            cols = pl.ds(pl.multiple_of(iz * 512, 512), 512)
            r0, r1 = right[0, :, cols], right[1, :, cols]
            for y in range(4):
                acc = jnp.dot(lhs[y, :, 0:ROWS], r0, preferred_element_type=f32)
                acc = acc + jnp.dot(lhs[y, :, ROWS:], r1, preferred_element_type=f32)
                acc = acc.astype(bf16)
                for ix in range(4):
                    where = {"z": iz, "x": ix, "y": y}
                    index = tuple(where[axis] for axis in ORDERS[k])
                    part[(k,) + index] = acc[:, ix * LANES:(ix + 1) * LANES]

    for one in w_near:
        one.finish()
    for one in w_far:
        one.start()
    ready(4)
    products(2, mk)
    rs[2][0].start()
    for one in w_far:
        one.middle()
    for one in w_far:
        one.finish()

    for s in range(2):
        @pl.loop(0, 4)
        def back_rows(t, s=s):
            k, sub = lax.div(t, 2), lax.rem(t, 2)
            rows = pl.ds(pl.multiple_of(t * 96, 96), 96)
            place = pl.ds(pl.multiple_of(sub * 96, 96), 96)
            which = rex[s, 0:1, :]
            right = mk[s]
            both = []
            for e in range(2):
                pieces = []
                for iz in range(4):
                    for ix in range(4):
                        pieces.append(wall[0, ix, iz, rows, :] if e == 0 else wall[1, iz, ix, rows, :])
                w = jnp.concatenate(pieces, axis=1)
                both.append(lax.dot_general(w, right, (((1,), (1,)), ((), ())), preferred_element_type=f32))
            back = jnp.where(which == 0, both[0], both[1])
            gate = gb[s, rows, :].astype(f32)
            upper = ub[s, rows, :].astype(f32)
            sig = jax.nn.sigmoid(gate)
            grads = (back * upper * sig * (1.0 + gate * (1.0 - sig)), back * gate * sig)
            for e in range(2):
                for h in range(2):
                    kept = jnp.where(which == e, grads[h], 0.0).astype(bf16)
                    left_side[k, 2 * e + h, place, s * ROWS:(s + 1) * ROWS] = kept

    ready(5)
    products(0, tk)
    rs[0][0].start()
    rs[2][0].middle()
    products(1, tk)
    rs[1][0].start()
    rs[2][0].finish()
    rs[2][1].start()
    rs[0][0].middle()
    rs[1][0].middle()
    rs[2][1].middle()
    rs[2][1].finish()
    rs[2][2].start()
    rs[2][2].middle()
    rs[2][2].finish()
    rs[0][0].finish()
    rs[0][1].start()
    rs[1][0].finish()
    rs[1][1].start()
    rs[0][1].middle()
    rs[1][1].middle()
    rs[0][1].finish()
    rs[0][2].start()
    rs[1][1].finish()
    rs[1][2].start()
    rs[0][2].middle()
    rs[1][2].middle()
    rs[0][2].finish()
    rs[1][2].finish()
    for k in range(3):
        order = ORDERS[k]
        a, b, d = (lax.axis_index(axis) for axis in order)
        out[k] = part[k, a, b, d]
    for copy in cross:
        copy.wait_send()
    for one in w_near + w_far:
        one.drain()
    for k in range(3):
        for one in rs[k]:
            one.drain()


def grad_sums(masked, tokens, gate_t, up_t, row_expert, w_pad):
    anywhere = pl.BlockSpec(memory_space=pl.ANY)
    vmem = pltpu.VMEM
    dma = pltpu.SemaphoreType.DMA
    return pl.pallas_call(
        grad_kernel,
        out_shape=jax.ShapeDtypeStruct((3, THIRD, LANES), bf16),
        in_specs=[anywhere] * 6,
        out_specs=pl.BlockSpec(memory_space=vmem),
        scratch_shapes=[
            vmem((2, ROWS, D), bf16),
            vmem((2, ROWS, D), bf16),
            vmem((2, HALF, ROWS), bf16),
            vmem((2, HALF, ROWS), bf16),
            vmem((2, 8, ROWS), f32),
            vmem((2, 2, HALF, LANES), bf16),
            vmem((2, 4, 4, HALF, LANES), bf16),
            vmem((3, 4, THIRD, 2 * ROWS), bf16),
            vmem((3, 4, 4, 4, THIRD, LANES), bf16),
            vmem((3, 4, 4, THIRD, LANES), bf16),
            vmem((3, 2, 4, 4, THIRD, LANES), bf16),
            vmem((3, 4, THIRD, LANES), bf16),
            vmem((3, 2, 4, THIRD, LANES), bf16),
            vmem((3, THIRD, LANES), bf16),
            vmem((3, 2, THIRD, LANES), bf16),
            dma((6,)),
            dma((6,)),
            dma((6,)),
            dma((4, 4)),
            dma((4, 4)),
            dma((3, 3, 6)),
            dma((3, 3, 6)),
        ],
        compiler_params=pltpu.CompilerParams(
            collective_id=0, has_side_effects=True, vmem_limit_bytes=60 * 1024 * 1024
        ),
        name="grad_sums",
    )(masked, tokens, gate_t, up_t, row_expert, w_pad)


GRAM_ROWS = F // 16


def newton_kernel(
    sums, out,
    pair, from_core, pair_core, mat, gram, whole, near0, fin0, near1, fin1,
    g1, p1, u, g2, p2,
    x_send, x_recv, g_send, g_recv, a_send, a_recv, o_send, o_recv,
):
    c, y = lax.axis_index("core"), lax.axis_index("y")
    h = lax.rem(y, 2)
    mate = y + 1 - 2 * h
    other = {"core": 1 - c}
    greet(AXES, True)
    down = push(sums.at[2], pair, x_send.at[0], x_recv.at[0], {"y": mate})
    swap = push(sums, from_core, x_send.at[1], x_recv.at[1], other)
    down.wait_recv()
    onward = push(pair, pair_core, x_send.at[2], x_recv.at[2], other)
    swap.wait_recv()
    onward.wait_recv()

    @pl.when(c == 0)
    def first_core():
        for k in range(2):
            mat[k] = sums[k]
            mat[2 + k] = from_core[k]

    @pl.when(c == 1)
    def second_core():
        mat[h] = from_core[2]
        mat[1 - h] = pair_core[...]
        mat[2 + h] = sums[2]
        mat[3 - h] = pair[...]

    X = jnp.concatenate([mat[k] for k in range(4)], axis=0)
    for a in range(4):
        block = lax.dot_general(mat[a], X, (((1,), (1,)), ((), ())), preferred_element_type=f32).astype(bf16)
        for b in range(4):
            for k in range(2):
                gram[k, a, b] = block[b * GRAM_ROWS:(b + 1) * GRAM_ROWS, k * HALF:(k + 1) * HALF]

    four = lead_halves(4)
    lanes = lane_halves(HALF, LANES)
    orders = (("z", "x"), ("x", "z"))
    rs0, rs1, ag0, ag1 = [], [], [], []
    for k in range(2):
        first_axis, second_axis = orders[k]
        a = lax.axis_index(first_axis)
        rs0.append(Scatter(first_axis, gram.at[k], *four, near0.at[k], fin0.at[k], g_send.at[k, 0], g_recv.at[k, 0], add_blocks))
        rs1.append(Scatter(second_axis, gram.at[k, a], *lanes, near1.at[k], fin1.at[k], g_send.at[k, 1], g_recv.at[k, 1], add_blocks))
        ag0.append(Gather(second_axis, whole.at[k, a], *lanes, a_send.at[k, 0], a_recv.at[k, 0]))
        ag1.append(Gather(first_axis, whole.at[k], *four, a_send.at[k, 1], a_recv.at[k, 1]))
    for k in range(2):
        rs0[k].start()
    for k in range(2):
        rs0[k].middle()
    for k in range(2):
        rs0[k].finish()
        rs1[k].start()
    for k in range(2):
        rs1[k].middle()
    for k in range(2):
        rs1[k].finish()
        a, b = (lax.axis_index(axis) for axis in orders[k])
        whole[k, a, b] = gram[k, a, b]
        ag0[k].start()
    for k in range(2):
        ag0[k].middle()
    for k in range(2):
        ag0[k].finish()
        ag1[k].start()
    for k in range(2):
        ag1[k].middle()
    for k in range(2):
        ag1[k].finish()

    trace = jnp.zeros((GRAM_ROWS, HALF), f32)
    row = lax.broadcasted_iota(jnp.int32, (GRAM_ROWS, HALF), 0)
    col = lax.broadcasted_iota(jnp.int32, (GRAM_ROWS, HALF), 1)
    for n in range(16):
        k, start = n // 8, (n % 8) * GRAM_ROWS
        trace = trace + jnp.where(col == row + start, whole[k, n // 4, n % 4].astype(f32), 0.0)
    squares = jnp.sum(jnp.sum(trace, axis=0, keepdims=True), axis=1, keepdims=True)
    scale = 1.0 / (jnp.sqrt(squares) + norm_eps)
    for n in range(16):
        for k in range(2):
            value = whole[k, n // 4, n % 4].astype(f32) * scale * scale
            g1[n * GRAM_ROWS:(n + 1) * GRAM_ROWS, k * HALF:(k + 1) * HALF] = value.astype(bf16)

    def rowwise(body):
        @pl.loop(0, 3)
        def one(t):
            body(pl.ds(pl.multiple_of(t * 256, 256), 256))

    def times(left, right):
        return jnp.dot(left, right[...], preferred_element_type=f32)

    def make_p1(rows):
        g = g1[rows, :]
        p1[rows, :] = (ns_second * g.astype(f32) + ns_third * times(g, g1)).astype(bf16)

    def make_u(rows):
        u[rows, :] = (ns_first * g1[rows, :].astype(f32) + times(p1[rows, :], g1)).astype(bf16)

    def make_g2(rows):
        g2[rows, :] = (ns_first * u[rows, :].astype(f32) + times(p1[rows, :], u)).astype(bf16)

    def make_p2(rows):
        g = g2[rows, :]
        p2[rows, :] = (ns_second * g.astype(f32) + ns_third * times(g, g2)).astype(bf16)

    factor = scale * jnp.sqrt(f32(D))

    def make_out(rows):
        p = p2[rows, :]
        r = ns_first * (p1[rows, :].astype(f32) + p.astype(f32)) + times(p, p1)
        u[rows, :] = r.astype(bf16)

    for body in (make_p1, make_u, make_g2, make_p2, make_out):
        rowwise(body)
    for n in range(4):
        rows = pl.ds(n * THIRD, THIRD)
        new = ns_first * ns_first * mat[n].astype(f32) + jnp.dot(u[rows, :], X, preferred_element_type=f32)
        out[c, y, rows, :] = (factor * new).astype(bf16)

    halves = lead_halves(F)
    ring = Gather("y", out.at[c], *halves, o_send.at[0], o_recv.at[0])
    i, right, left, far = around("y")
    over = [push(out.at[c, i], out.at[c, i], x_send.at[3], x_recv.at[3], other)]
    ring.start()
    ring.middle()
    over.append(push(out.at[c, left], out.at[c, left], x_send.at[4], x_recv.at[4], other))
    over.append(push(out.at[c, right], out.at[c, right], x_send.at[5], x_recv.at[5], other))
    ring.finish()
    over.append(push(out.at[c, far], out.at[c, far], x_send.at[6], x_recv.at[6], other))
    for copy in over:
        copy.wait_recv()
    for copy in [down, swap, onward] + over:
        copy.wait_send()
    for one in rs0 + rs1 + ag0 + ag1 + [ring]:
        one.drain()


def newton(sums):
    vmem = pltpu.VMEM
    dma = pltpu.SemaphoreType.DMA
    square = vmem((F, F), bf16)
    return pl.pallas_call(
        newton_kernel,
        out_shape=jax.ShapeDtypeStruct((2, 4, F, LANES), bf16),
        in_specs=[pl.BlockSpec(memory_space=vmem)],
        out_specs=pl.BlockSpec(memory_space=vmem),
        scratch_shapes=[
            vmem((THIRD, LANES), bf16),
            vmem((3, THIRD, LANES), bf16),
            vmem((THIRD, LANES), bf16),
            vmem((4, THIRD, LANES), bf16),
            vmem((2, 4, 4, GRAM_ROWS, HALF), bf16),
            vmem((2, 4, 4, GRAM_ROWS, HALF), bf16),
            vmem((2, 4, GRAM_ROWS, HALF), bf16),
            vmem((2, 2, 4, GRAM_ROWS, HALF), bf16),
            vmem((2, GRAM_ROWS, HALF), bf16),
            vmem((2, 2, GRAM_ROWS, HALF), bf16),
            square, square, square, square, square,
            dma((7,)),
            dma((7,)),
            dma((2, 2, 6)),
            dma((2, 2, 6)),
            dma((2, 2, 4)),
            dma((2, 2, 4)),
            dma((1, 4)),
            dma((1, 4)),
        ],
        compiler_params=pltpu.CompilerParams(
            collective_id=1, has_side_effects=True, vmem_limit_bytes=60 * 1024 * 1024
        ),
        name="newton",
    )(sums)


def per_device(
    token_inputs, cotangent, gate_preact, up_preact, down_weight, block_expert, block_count
):
    blocks = block_count.shape[0]
    rows_here = token_inputs.shape[0]
    block_rows = rows_here // blocks
    c = lax.axis_index("core")
    row_place = jnp.arange(rows_here, dtype=jnp.int32) % block_rows
    row_count = jnp.repeat(block_count, block_rows, total_repeat_length=rows_here)
    masked = jnp.where((row_place < row_count)[:, None], cotangent, jnp.zeros_like(cotangent))
    row_expert = jnp.repeat(block_expert, block_rows, total_repeat_length=rows_here).astype(f32)
    row_expert = jnp.broadcast_to(row_expert[None, :], (8, rows_here))
    gate_t = gate_preact.T.reshape(2, HALF, rows_here)
    up_t = up_preact.T.reshape(2, HALF, rows_here)
    cols = down_weight.shape[2]
    lane = jnp.arange(2 * cols, dtype=jnp.int32) // cols
    w_pad = jnp.concatenate([down_weight, down_weight], axis=2)
    w_pad = jnp.where(lane[None, None, :] == c, w_pad, jnp.zeros_like(w_pad))
    w_pad = w_pad.reshape(2, 2, HALF, 2 * cols).swapaxes(0, 1)
    sums = grad_sums(masked, token_inputs, gate_t, up_t, row_expert, w_pad)
    done = newton(sums)
    mine = lax.dynamic_slice_in_dim(done, c * cols, cols, 3)
    top = mine[0].reshape(2, 2, F, cols)
    low = mine[1].reshape(2, 2, F, cols)[:, :1]
    return jnp.concatenate([top, low], axis=1)


def solution(mesh):
    torus = Mesh(mesh.devices.reshape(4, 4, 2, mesh.shape["rep"]), ("z", "x", "core", "y"))
    dp, dp_rep = ("z", "x", "core"), ("z", "x", "core", "y")
    return jax.shard_map(
        per_device,
        mesh=torus,
        in_specs=(
            P(dp_rep, None),
            P(dp_rep, None),
            P(dp_rep, None),
            P(dp_rep, None),
            P(None, None, dp),
            P(dp_rep),
            P(dp_rep),
        ),
        out_specs=P(None, None, None, dp),
        check_vma=False,
    )
```

```python
import functools

import jax
import jax.numpy as jnp
from jax import lax
from jax.experimental import pallas as pl
from jax.experimental.pallas import tpu as pltpu
from jax.sharding import Mesh
from jax.sharding import PartitionSpec as P

D = 2048
F = 768
ROWS = 512
BLOCK = 128
HALF = F // 2
THIRD = HALF // 2
LANES = 128
AXES = ("z", "x", "y")
UNITS = (
    (0, 128, ("x", "z", "y"), False),
    (128, 128, ("y", "x", "z"), False),
    (256, 64, ("z", "x", "y"), False),
    (320, 64, ("z", "y", "x"), False),
    (0, 128, ("y", "z", "x"), True),
    (128, 64, ("y", "x", "z"), True),
)
STEPS = (
    ("hid", 0, ""),
    ("wn", 0, "m"),
    ("wn", 1, "m"),
    ("pd", 0, ""),
    ("wn", 0, "f"),
    ("wn", 1, "f"),
    (4, 0, "m"),
    ("wf", 0, "m"),
    ("wf", 1, "m"),
    (5, 0, "m"),
    ("wf", 0, "f"),
    ("wf", 1, "f"),
    ("wfull", 0, ""),
    ("back", 0, ""),
    ("p0", 0, ""),
    (4, 0, "f"),
    (5, 0, "f"),
    ("p1", 0, ""),
    (4, 1, "m"),
    ("p2", 0, ""),
    ("p3", 0, ""),
    (0, 0, "m"),
    (4, 1, "f"),
    (2, 0, "m"),
    (1, 0, "m"),
    (5, 1, "m"),
    (3, 0, "m"),
    (0, 0, "f"),
    (4, 2, "m"),
    (5, 1, "f"),
    (2, 0, "f"),
    (4, 2, "f"),
    (1, 0, "f"),
    (2, 1, "m"),
    (3, 0, "f"),
    (0, 1, "m"),
    (1, 1, "m"),
    (3, 1, "m"),
    (5, 2, "m"),
    (2, 1, "f"),
    (0, 1, "f"),
    (5, 2, "f"),
    (3, 1, "f"),
    (1, 1, "f"),
    (2, 2, "m"),
    (0, 2, "m"),
    (3, 2, "m"),
    (1, 2, "m"),
    (2, 2, "f"),
    (0, 2, "f"),
    (3, 2, "f"),
    (1, 2, "f"),
)
MESH = pl.DeviceIdType.MESH

ns_first = 3.4445
ns_second = -4.775
ns_third = 2.0315
norm_eps = 1e-07

bf16 = jnp.bfloat16
f32 = jnp.float32


def around(axis):
    i = lax.axis_index(axis)
    return i, lax.rem(i + 1, 4), lax.rem(i + 3, 4), lax.rem(i + 2, 4)


def push(src, dst, send, recv, device):
    copy = pltpu.make_async_remote_copy(
        src_ref=src, dst_ref=dst, send_sem=send, recv_sem=recv, device_id=device, device_id_type=MESH
    )
    copy.start()
    return copy


def greet(axes, others):
    barrier = pltpu.get_barrier_semaphore()
    count = 0
    for axis in axes:
        i, right, left, far = around(axis)
        for other in (right, left):
            pl.semaphore_signal(barrier, inc=1, device_id={axis: other}, device_id_type=MESH)
            count += 1
    for device in others:
        pl.semaphore_signal(barrier, inc=1, device_id=device, device_id_type=MESH)
        count += 1
    pl.semaphore_wait(barrier, count)


class Scatter:
    def __init__(self, axis, src, first, second, near, final, send, recv, add):
        self.axis, self.src, self.first, self.second = axis, src, first, second
        self.near, self.final, self.send, self.recv, self.add = near, final, send, recv, add

    def start(self):
        i, right, left, far = around(self.axis)
        src, first, second, send, recv = self.src, self.first, self.second, self.send, self.recv
        to_right, to_left = {self.axis: right}, {self.axis: left}
        self.a1 = push(first(src.at[far]), first(self.near), send.at[0], recv.at[0], to_right)
        self.b1 = push(second(src.at[far]), second(self.near), send.at[1], recv.at[1], to_left)
        self.a2 = push(second(src.at[right]), second(self.final.at[0]), send.at[2], recv.at[2], to_right)
        self.b2 = push(first(src.at[left]), first(self.final.at[1]), send.at[3], recv.at[3], to_left)

    def middle(self):
        i, right, left, far = around(self.axis)
        src, first, second, send, recv = self.src, self.first, self.second, self.send, self.recv
        self.a1.wait_recv()
        self.add(first(src.at[right]), (first(self.near),))
        self.a3 = push(first(src.at[right]), first(self.final.at[0]), send.at[4], recv.at[4], {self.axis: right})
        self.b1.wait_recv()
        self.add(second(src.at[left]), (second(self.near),))
        self.b3 = push(second(src.at[left]), second(self.final.at[1]), send.at[5], recv.at[5], {self.axis: left})

    def finish(self):
        i, right, left, far = around(self.axis)
        for copy in (self.a2, self.b2, self.a3, self.b3):
            copy.wait_recv()
        self.add(self.src.at[i], (self.final.at[0], self.final.at[1]))

    def drain(self):
        for copy in (self.a1, self.b1, self.a2, self.b2, self.a3, self.b3):
            copy.wait_send()


class Gather:
    def __init__(self, axis, buf, first, second, send, recv):
        self.axis, self.buf, self.first, self.second = axis, buf, first, second
        self.send, self.recv = send, recv

    def start(self):
        i, right, left, far = around(self.axis)
        buf = self.buf
        self.a1 = push(buf.at[i], buf.at[i], self.send.at[0], self.recv.at[0], {self.axis: right})
        self.b1 = push(buf.at[i], buf.at[i], self.send.at[1], self.recv.at[1], {self.axis: left})

    def middle(self):
        i, right, left, far = around(self.axis)
        buf, first, second = self.buf, self.first, self.second
        self.a1.wait_recv()
        self.a2 = push(first(buf.at[left]), first(buf.at[left]), self.send.at[2], self.recv.at[2], {self.axis: right})
        self.b1.wait_recv()
        self.b2 = push(second(buf.at[right]), second(buf.at[right]), self.send.at[3], self.recv.at[3], {self.axis: left})

    def finish(self):
        self.a2.wait_recv()
        self.b2.wait_recv()

    def drain(self):
        for copy in (self.a1, self.b1, self.a2, self.b2):
            copy.wait_send()


def add_blocks(dst, others):
    lead = dst.shape[:-2]
    count = 1
    for size in lead:
        count *= size

    def one(n, carry):
        index = []
        rest = n
        for size in reversed(lead):
            index.append(lax.rem(rest, size))
            rest = lax.div(rest, size)
        index = tuple(reversed(index))
        total = dst[index].astype(f32)
        for other in others:
            total = total + other[index].astype(f32)
        dst[index] = total.astype(bf16)
        return carry

    if count == 1:
        one(0, 0)
    else:
        lax.fori_loop(0, count, one, 0)


def lead_halves(size):
    half = size // 2
    return (lambda ref: ref.at[pl.ds(0, half)]), (lambda ref: ref.at[pl.ds(half, half)])


NT = (((1,), (1,)), ((), ()))


def grad_kernel(
    experts, counts, cotangent, tokens, gate, up, weight_t, out,
    mk, tk, gb, ub, gt, ut, rex, wx, wall, wfull, back_ref, left_g, left_d, *rest
):
    own_sem, x_send, x_recv, w_send, w_recv, r_send, r_recv = rest[-7:]
    buffers = [rest[7 * k:7 * k + 7] for k in range(len(UNITS))]
    c = lax.axis_index("core")
    other = {"core": 1 - c}
    mine = pl.ds(pl.multiple_of(c * HALF, HALF), HALF)
    theirs = pl.ds(pl.multiple_of((1 - c) * HALF, HALF), HALF)
    own = []
    for n, (src, dst) in enumerate((
        (weight_t.at[:, :, mine], wx.at[c]),
        (gate.at[:, mine], gb.at[0]),
        (up.at[:, mine], ub.at[0]),
        (cotangent, mk.at[0]),
        (tokens, tk.at[0]),
    )):
        copy = pltpu.make_async_copy(src, dst, own_sem.at[n])
        copy.start()
        own.append(copy)
    lane = lax.broadcasted_iota(jnp.int32, (8, BLOCK), 1)
    for b in range(ROWS // BLOCK):
        code = jnp.where(lane < counts[b], experts[b], 2)
        rex[0, :, b * BLOCK:(b + 1) * BLOCK] = code.astype(f32)
    greet(AXES, (other,))
    cross = []
    for n, (src, dst) in enumerate((
        (weight_t.at[:, :, theirs], wx.at[c]),
        (gate.at[:, theirs], gb.at[1]),
        (up.at[:, theirs], ub.at[1]),
        (cotangent, mk.at[1]),
        (tokens, tk.at[1]),
        (rex.at[0], rex.at[1]),
    )):
        cross.append(push(src, dst, x_send.at[n], x_recv.at[n], other))

    def ready(n):
        if n < 5:
            own[n].wait()
        cross[n].wait_recv()

    z, x = lax.axis_index("z"), lax.axis_index("x")
    first, second = lead_halves(HALF)
    four_first, four_second = lead_halves(4)
    w_near = [
        Gather("z", wall.at[0, x], first, second, w_send.at[0], w_recv.at[0]),
        Gather("x", wall.at[1, z], first, second, w_send.at[1], w_recv.at[1]),
    ]
    w_far = [
        Gather("x", wall.at[0], four_first, four_second, w_send.at[2], w_recv.at[2]),
        Gather("z", wall.at[1], four_first, four_second, w_send.at[3], w_recv.at[3]),
    ]
    ready(0)
    for e in range(2):
        block = jnp.concatenate([wx[0, e], wx[1, e]], axis=0).astype(f32).T.astype(bf16)
        if e == 0:
            wall[0, x, z] = block
        else:
            wall[1, z, x] = block
    for one in w_near:
        one.start()

    rs = []
    cut = lead_halves(4)
    for k, (start, rows, order, down) in enumerate(UNITS):
        a, b = lax.axis_index(order[0]), lax.axis_index(order[1])
        part, near0, fin0, near1, fin1, near2, fin2 = buffers[k]
        rs.append(
            (
                Scatter(order[0], part, *cut, near0, fin0, r_send.at[k, 0], r_recv.at[k, 0], add_blocks),
                Scatter(order[1], part.at[a], *cut, near1, fin1, r_send.at[k, 1], r_recv.at[k, 1], add_blocks),
                Scatter(order[2], part.at[a, b], *lead_halves(rows), near2, fin2, r_send.at[k, 2], r_recv.at[k, 2], add_blocks),
            )
        )

    def make_hidden():
        for n in (1, 2, 5):
            ready(n)
        for s in range(2):
            @pl.loop(0, ROWS // BLOCK)
            def hidden_rows(t, s=s):
                rows = pl.ds(pl.multiple_of(t * BLOCK, BLOCK), BLOCK)
                there = pl.ds(pl.multiple_of(s * ROWS + t * BLOCK, BLOCK), BLOCK)
                g = gb[s, rows, :].astype(f32).T
                u = ub[s, rows, :].astype(f32).T
                gt[s, :, rows] = g.astype(bf16)
                ut[s, :, rows] = u.astype(bf16)
                hidden = g * jax.nn.sigmoid(g) * u
                which = rex[s, 0:1, rows]
                for e in range(2):
                    kept = jnp.where(which == e, hidden, 0.0).astype(bf16)
                    for h in range(2):
                        left_d[2 * e + h, :, there] = kept[h * THIRD:(h + 1) * THIRD]

    def products(picked):
        down = UNITS[picked[0]][3]
        lhs_ref, right = (left_d, mk) if down else (left_g, tk)
        low = UNITS[picked[0]][0]
        size = sum(UNITS[k][1] for k in picked)

        @pl.loop(0, 4)
        def columns(iz):
            cols = pl.ds(pl.multiple_of(iz * 512, 512), 512)
            lhs = lhs_ref[:, low:low + size, :].reshape(4 * size, 2 * ROWS)
            rhs = right[:, :, cols].reshape(2 * ROWS, 512)
            acc = jnp.dot(lhs, rhs, preferred_element_type=f32).astype(bf16)
            for k in picked:
                start, rows, order, _ = UNITS[k]
                for y in range(4):
                    first = y * size + start - low
                    for ix in range(4):
                        where = {"z": iz, "x": ix, "y": y}
                        index = tuple(where[axis] for axis in order)
                        buffers[k][0][index] = acc[first:first + rows, ix * LANES:(ix + 1) * LANES]

        for k in picked:
            rs[k][0].start()

    def pack_weights():
        for iz in range(4):
            for ix in range(4):
                cols = slice((iz * 4 + ix) * LANES, (iz * 4 + ix + 1) * LANES)
                wfull[0:HALF, cols] = wall[0, ix, iz]
                wfull[HALF:, cols] = wall[1, iz, ix]

    def make_back():
        tile = 32
        for s in range(2):
            @pl.loop(0, 2)
            def back_columns(t, s=s):
                rows = pl.ds(pl.multiple_of(t * 256, 256), 256)
                back_ref[:, rows] = lax.dot_general(wfull[...], mk[s, rows, :], NT, preferred_element_type=f32)

            @pl.loop(0, HALF // tile)
            def back_rows(t, s=s):
                rows = pl.ds(pl.multiple_of(t * tile, tile), tile)
                low = pl.ds(pl.multiple_of(HALF + t * tile, tile), tile)
                which = rex[s, 0:1, :]
                back = jnp.where(which == 0, back_ref[rows, :], back_ref[low, :])
                g = gt[s, rows, :].astype(f32)
                u = ut[s, rows, :].astype(f32)
                sig = jax.nn.sigmoid(g)
                grads = (back * u * sig * (1.0 + g * (1.0 - sig)), back * g * sig)
                for e in range(2):
                    for h in range(2):
                        kept = jnp.where(which == e, grads[h], 0.0).astype(bf16)
                        left_g[2 * e + h, rows, s * ROWS:(s + 1) * ROWS] = kept

    def advance(unit, phase, what):
        if what == "m":
            rs[unit][phase].middle()
        else:
            rs[unit][phase].finish()
            if phase < 2:
                rs[unit][phase + 1].start()

    for name, e, what in STEPS:
        if name == "hid":
            make_hidden()
        elif name == "pd":
            ready(3)
            products([k for k in range(len(UNITS)) if UNITS[k][3]])
        elif name == "wfull":
            pack_weights()
        elif name == "back":
            make_back()
            ready(4)
        elif name == "wn":
            if what == "m":
                w_near[e].middle()
            else:
                w_near[e].finish()
                w_far[e].start()
        elif name == "wf":
            if what == "m":
                w_far[e].middle()
            else:
                w_far[e].finish()
        elif isinstance(name, str):
            products([int(name[1:])])
        else:
            advance(name, e, what)
    for k, (start, rows, order, down) in enumerate(UNITS):
        a, b, d = (lax.axis_index(axis) for axis in order)
        start = start + (HALF if down else 0)
        out[start:start + rows, :] = buffers[k][0][a, b, d]
    for copy in cross:
        copy.wait_send()
    for one in w_near + w_far:
        one.drain()
    for unit in rs:
        for one in unit:
            one.drain()


def grad_sums(experts, counts, cotangent, tokens, gate, up, weight_t):
    anywhere = pl.BlockSpec(memory_space=pl.ANY)
    smem = pl.BlockSpec(memory_space=pltpu.SMEM)
    vmem = pltpu.VMEM
    dma = pltpu.SemaphoreType.DMA
    buffers = []
    for start, rows, order, down in UNITS:
        block = (rows, LANES)
        for lead in ((4, 4, 4), (4, 4), (2, 4, 4), (4,), (2, 4), (), (2,)):
            buffers.append(vmem(lead + block, bf16))
    return pl.pallas_call(
        grad_kernel,
        out_shape=jax.ShapeDtypeStruct((3 * THIRD, LANES), bf16),
        in_specs=[smem] * 2 + [anywhere] * 5,
        out_specs=pl.BlockSpec(memory_space=vmem),
        scratch_shapes=[
            vmem((2, ROWS, D), bf16),
            vmem((2, ROWS, D), bf16),
            vmem((2, ROWS, HALF), bf16),
            vmem((2, ROWS, HALF), bf16),
            vmem((2, HALF, ROWS), bf16),
            vmem((2, HALF, ROWS), bf16),
            vmem((2, 8, ROWS), f32),
            vmem((2, 2, LANES // 2, HALF), bf16),
            vmem((2, 4, 4, HALF, LANES), bf16),
            vmem((F, D), bf16),
            vmem((F, ROWS), f32),
            vmem((4, HALF, 2 * ROWS), bf16),
            vmem((4, THIRD, 2 * ROWS), bf16),
            *buffers,
            dma((5,)),
            dma((6,)),
            dma((6,)),
            dma((4, 4)),
            dma((4, 4)),
            dma((len(UNITS), 3, 6)),
            dma((len(UNITS), 3, 6)),
        ],
        compiler_params=pltpu.CompilerParams(
            collective_id=0, has_side_effects=True, vmem_limit_bytes=62 * 1024 * 1024
        ),
        name="grad_sums",
    )(experts, counts, cotangent, tokens, gate, up, weight_t)


CHUNK = 96
PAIRS = ((0, 0), (0, 1), (0, 2), (1, 1), (1, 2), (2, 2))
WIDE = 256
STRIP = 32


def strips():
    for n in range(len(PAIRS) * WIDE // STRIP):
        row = n * STRIP
        yield n // 8, (n % 8) * STRIP, row // CHUNK, row % CHUNK


def newton_kernel(
    sums, out,
    pair, from_core, pair_core, mat, gram, whole, near0, fin0, near1, fin1,
    g1, p1, u, g2, p2, ring0, ring1,
    x_send, x_recv, g_send, g_recv, a_send, a_recv, o_send, o_recv,
):
    c, y = lax.axis_index("core"), lax.axis_index("y")
    h = lax.rem(y, 2)
    mate = y + 1 - 2 * h
    other = {"core": 1 - c}
    greet(AXES, (other, {"y": mate, "core": 1 - c}))
    low_rows = sums.at[pl.ds(HALF, THIRD)]
    down = push(low_rows, pair, x_send.at[0], x_recv.at[0], {"y": mate})
    onward = push(low_rows, pair_core, x_send.at[2], x_recv.at[2], {"y": mate, "core": 1 - c})
    swap = push(sums, from_core, x_send.at[1], x_recv.at[1], other)
    for copy in (swap, down, onward):
        copy.wait_recv()

    @pl.when(c == 0)
    def first_core():
        for k in range(2):
            mat[k] = sums[k * THIRD:(k + 1) * THIRD]
            mat[2 + k] = from_core[k * THIRD:(k + 1) * THIRD]

    @pl.when(c == 1)
    def second_core():
        mat[h] = from_core[HALF:]
        mat[1 - h] = pair_core[...]
        mat[2 + h] = sums[HALF:]
        mat[3 - h] = pair[...]

    X = mat[...].reshape(F, LANES)
    blocks = []
    for i, j in PAIRS:
        left, right = X[i * WIDE:(i + 1) * WIDE], X[j * WIDE:(j + 1) * WIDE]
        blocks.append(lax.dot_general(left, right, NT, preferred_element_type=f32).astype(bf16))
    for n, rows, chunk, place in strips():
        for k in range(2):
            gram[k, chunk // 4, chunk % 4, place:place + STRIP, :] = blocks[n][
                rows:rows + STRIP, k * LANES:(k + 1) * LANES
            ]

    four = lead_halves(4)
    halves = lead_halves(CHUNK)
    orders = (("z", "x"), ("x", "z"))
    rs0, rs1, ag0, ag1 = [], [], [], []
    for k in range(2):
        first_axis, second_axis = orders[k]
        a = lax.axis_index(first_axis)
        rs0.append(Scatter(first_axis, gram.at[k], *four, near0.at[k], fin0.at[k], g_send.at[k, 0], g_recv.at[k, 0], add_blocks))
        rs1.append(Scatter(second_axis, gram.at[k, a], *halves, near1.at[k], fin1.at[k], g_send.at[k, 1], g_recv.at[k, 1], add_blocks))
        ag0.append(Gather(second_axis, whole.at[k, a], *halves, a_send.at[k, 0], a_recv.at[k, 0]))
        ag1.append(Gather(first_axis, whole.at[k], *four, a_send.at[k, 1], a_recv.at[k, 1]))
    for k in range(2):
        rs0[k].start()
    for k in range(2):
        rs0[k].middle()
    for k in range(2):
        rs0[k].finish()
        rs1[k].start()
    for k in range(2):
        rs1[k].middle()
    for k in range(2):
        rs1[k].finish()
        a, b = (lax.axis_index(axis) for axis in orders[k])
        whole[k, a, b] = gram[k, a, b]
        ag0[k].start()
    for k in range(2):
        ag0[k].middle()
    for k in range(2):
        ag0[k].finish()
        ag1[k].start()
    for k in range(2):
        ag1[k].middle()
    for k in range(2):
        ag1[k].finish()

    trace = jnp.zeros((STRIP, LANES), f32)
    row = lax.broadcasted_iota(jnp.int32, (STRIP, LANES), 0)
    col = lax.broadcasted_iota(jnp.int32, (STRIP, LANES), 1)
    for n, rows, chunk, place in strips():
        if PAIRS[n][0] == PAIRS[n][1]:
            k = rows // LANES
            value = whole[k, chunk // 4, chunk % 4, place:place + STRIP, :].astype(f32)
            trace = trace + jnp.where(col == row + rows % LANES, value, 0.0)
    squares = jnp.sum(jnp.sum(trace, axis=0, keepdims=True), axis=1, keepdims=True)
    scale = 1.0 / (jnp.sqrt(squares) + norm_eps)
    for n, rows, chunk, place in strips():
        i, j = PAIRS[n]
        for k in range(2):
            value = whole[k, chunk // 4, chunk % 4, place:place + STRIP, :].astype(f32) * scale * scale
            g1[i * WIDE + rows:i * WIDE + rows + STRIP, j * WIDE + k * LANES:j * WIDE + (k + 1) * LANES] = value.astype(bf16)
    for i, j in PAIRS:
        if i != j:
            block = g1[i * WIDE:(i + 1) * WIDE, j * WIDE:(j + 1) * WIDE]
            g1[j * WIDE:(j + 1) * WIDE, i * WIDE:(i + 1) * WIDE] = block.astype(f32).T.astype(bf16)

    def times(left, right, cols):
        return jnp.dot(left[...], right[:, cols], preferred_element_type=f32)

    def make_p1(cols):
        p1[:, cols] = (ns_second * g1[:, cols].astype(f32) + ns_third * times(g1, g1, cols)).astype(bf16)

    def make_u(cols):
        u[:, cols] = (ns_first * g1[:, cols].astype(f32) + times(p1, g1, cols)).astype(bf16)

    def make_g2(cols):
        g2[:, cols] = (ns_first * u[:, cols].astype(f32) + times(p1, u, cols)).astype(bf16)

    def make_p2(cols):
        p2[:, cols] = (ns_second * g2[:, cols].astype(f32) + ns_third * times(g2, g2, cols)).astype(bf16)

    def make_rest(cols):
        rest = ns_first * (p1[:, cols].astype(f32) + p2[:, cols].astype(f32)) + times(p2, p1, cols)
        u[:, cols] = rest.astype(bf16)

    for body in (make_p1, make_u, make_g2, make_p2, make_rest):
        @pl.loop(0, F // WIDE)
        def one(t, body=body):
            body(pl.ds(pl.multiple_of(t * WIDE, WIDE), WIDE))

    factor = scale * jnp.sqrt(f32(D))
    XT = X.astype(f32).T
    low = XT.astype(bf16)
    i, right, left, far = around("y")
    side = LANES // 2

    @pl.when(c == 0)
    def send_first():
        new = ns_first * ns_first * XT + jnp.dot(low, u[...], preferred_element_type=f32)
        ring0[i] = (factor * new).astype(bf16)
        ring = Gather("y", ring0, *lead_halves(LANES), o_send.at[0], o_recv.at[0])
        place = lambda t: out.at[lax.div(t, 2), lax.rem(t, 2)]
        give = lambda t, n: push(ring0.at[t, pl.ds(side, side)], place(t), x_send.at[n], x_recv.at[n], other)
        ring.start()
        over = [give(i, 3)]
        ring.middle()
        over.append(give(left, 4))
        over.append(give(right, 5))
        ring.finish()
        over.append(give(far, 6))
        for t in range(4):
            out[t // 2, t % 2] = ring0[t, 0:side]
        for n, t in enumerate((i, left, right, far)):
            span = pl.ds(pl.multiple_of(lax.rem(t, 2) * HALF, HALF), HALF)
            expected = out.at[lax.div(t, 2), 2, :, span]
            pltpu.make_async_remote_copy(
                src_ref=expected, dst_ref=expected, send_sem=x_send.at[3 + n], recv_sem=x_recv.at[3 + n],
                device_id=other, device_id_type=MESH,
            ).wait_recv()
        for copy in over:
            copy.wait_send()
        ring.drain()

    @pl.when(c == 1)
    def send_second():
        half = pl.ds(pl.multiple_of(h * HALF, HALF), HALF)
        g2[0:LANES, 0:HALF] = jnp.where(h == 0, XT[:, 0:HALF], XT[:, HALF:]).astype(bf16)
        new = ns_first * ns_first * g2[0:LANES, 0:HALF].astype(f32) + jnp.dot(
            low, u[:, half], preferred_element_type=f32
        )
        ring1[i] = (factor * new).astype(bf16)
        ring = Gather("y", ring1, *lead_halves(LANES), o_send.at[1], o_recv.at[1])
        place = lambda t: out.at[lax.div(t, 2), 2, :, pl.ds(pl.multiple_of(lax.rem(t, 2) * HALF, HALF), HALF)]
        give = lambda t, n: push(ring1.at[t, pl.ds(0, side)], place(t), x_send.at[n], x_recv.at[n], other)
        ring.start()
        over = [give(i, 3)]
        ring.middle()
        over.append(give(left, 4))
        over.append(give(right, 5))
        ring.finish()
        over.append(give(far, 6))
        for t in range(4):
            out[t // 2, 2, :, (t % 2) * HALF:(t % 2 + 1) * HALF] = ring1[t, side:]
        for n, t in enumerate((i, left, right, far)):
            expected = out.at[lax.div(t, 2), lax.rem(t, 2)]
            pltpu.make_async_remote_copy(
                src_ref=expected, dst_ref=expected, send_sem=x_send.at[3 + n], recv_sem=x_recv.at[3 + n],
                device_id=other, device_id_type=MESH,
            ).wait_recv()
        for copy in over:
            copy.wait_send()
        ring.drain()

    for copy in (down, swap, onward):
        copy.wait_send()
    for one in rs0 + rs1 + ag0 + ag1:
        one.drain()


def newton(sums):
    vmem = pltpu.VMEM
    dma = pltpu.SemaphoreType.DMA
    square = vmem((F, F), bf16)
    return pl.pallas_call(
        newton_kernel,
        out_shape=jax.ShapeDtypeStruct((2, 3, LANES // 2, F), bf16),
        in_specs=[pl.BlockSpec(memory_space=vmem)],
        out_specs=pl.BlockSpec(memory_space=vmem),
        scratch_shapes=[
            vmem((THIRD, LANES), bf16),
            vmem((3 * THIRD, LANES), bf16),
            vmem((THIRD, LANES), bf16),
            vmem((4, THIRD, LANES), bf16),
            vmem((2, 4, 4, CHUNK, LANES), bf16),
            vmem((2, 4, 4, CHUNK, LANES), bf16),
            vmem((2, 4, CHUNK, LANES), bf16),
            vmem((2, 2, 4, CHUNK, LANES), bf16),
            vmem((2, CHUNK, LANES), bf16),
            vmem((2, 2, CHUNK, LANES), bf16),
            square, square, square, square, square,
            vmem((4, LANES, F), bf16),
            vmem((4, LANES, HALF), bf16),
            dma((7,)),
            dma((7,)),
            dma((2, 2, 6)),
            dma((2, 2, 6)),
            dma((2, 2, 4)),
            dma((2, 2, 4)),
            dma((2, 4)),
            dma((2, 4)),
        ],
        compiler_params=pltpu.CompilerParams(
            collective_id=1, has_side_effects=True, vmem_limit_bytes=60 * 1024 * 1024
        ),
        name="newton",
    )(sums)


def per_device(
    token_inputs, cotangent, gate_preact, up_preact, down_weight, block_expert, block_count
):
    sums = grad_sums(
        block_expert, block_count, cotangent, token_inputs, gate_preact, up_preact,
        down_weight.swapaxes(1, 2),
    )
    return newton(sums).swapaxes(2, 3)


def solution(mesh):
    torus = Mesh(mesh.devices.reshape(4, 4, 2, mesh.shape["rep"]), ("z", "x", "core", "y"))
    dp, dp_rep = ("z", "x", "core"), ("z", "x", "core", "y")
    return jax.shard_map(
        per_device,
        mesh=torus,
        in_specs=(
            P(dp_rep, None),
            P(dp_rep, None),
            P(dp_rep, None),
            P(dp_rep, None),
            P(None, None, dp),
            P(dp_rep),
            P(dp_rep),
        ),
        out_specs=P(None, None, None, dp),
        check_vma=False,
    )
```

```python
import functools

import jax
import jax.numpy as jnp
from jax import lax
from jax.experimental import pallas as pl
from jax.experimental.pallas import tpu as pltpu
from jax.sharding import Mesh
from jax.sharding import PartitionSpec as P

D = 2048
F = 768
ROWS = 512
BLOCK = 128
HALF = F // 2
THIRD = HALF // 2
LANES = 128
AXES = ("z", "x", "y")
UNITS = (
    (0, 64, ("x", "y", "z"), False),
    (64, 64, ("y", "z", "x"), False),
    (128, 64, ("z", "y", "x"), False),
    (192, 64, ("y", "x", "z"), False),
    (256, 64, ("z", "y", "x"), False),
    (320, 64, ("x", "z", "y"), False),
    (0, 192, ("y", "x", "z"), True),
)
STEPS = (
    ("hid", 0, ""),
    ("pd", 0, ""),
    ("wn", 0, "m"),
    ("wn", 1, "m"),
    ("wn", 0, "f"),
    ("wn", 1, "f"),
    (6, 0, "m"),
    ("wf", 0, "m"),
    ("wf", 1, "m"),
    ("wf", 0, "f"),
    ("wf", 1, "f"),
    ("wfull", 0, ""),
    ("back", 0, ""),
    ("prod", 0, ""),
    ("prod", 1, ""),
    ("back", 128, ""),
    ("prod", 2, ""),
    (0, 0, "m"),
    (6, 0, "f"),
    ("prod", 3, ""),
    (1, 0, "m"),
    ("back", 256, ""),
    (2, 0, "m"),
    (0, 0, "f"),
    ("prod", 4, ""),
    (3, 0, "m"),
    (6, 1, "m"),
    ("prod", 5, ""),
    (2, 0, "f"),
    (6, 1, "f"),
    (1, 0, "f"),
    (4, 0, "m"),
    (0, 1, "m"),
    (5, 0, "m"),
    (6, 2, "m"),
    (3, 0, "f"),
    (1, 1, "m"),
    (2, 1, "m"),
    (0, 1, "f"),
    (2, 1, "f"),
    (5, 0, "f"),
    (4, 0, "f"),
    (3, 1, "m"),
    (6, 2, "f"),
    ("low", 0, ""),
    (2, 2, "m"),
    (1, 1, "f"),
    (0, 2, "m"),
    (5, 1, "m"),
    (4, 1, "m"),
    (3, 1, "f"),
    (2, 2, "f"),
    (0, 2, "f"),
    (1, 2, "m"),
    (5, 1, "f"),
    (3, 2, "m"),
    (4, 1, "f"),
    (1, 2, "f"),
    (5, 2, "m"),
    (3, 2, "f"),
    (4, 2, "m"),
    (5, 2, "f"),
    (4, 2, "f"),
)
MESH = pl.DeviceIdType.MESH

ns_first = 3.4445
ns_second = -4.775
ns_third = 2.0315
norm_eps = 1e-07

bf16 = jnp.bfloat16
f32 = jnp.float32


def around(axis):
    i = lax.axis_index(axis)
    return i, lax.rem(i + 1, 4), lax.rem(i + 3, 4), lax.rem(i + 2, 4)


def push(src, dst, send, recv, device):
    copy = pltpu.make_async_remote_copy(
        src_ref=src, dst_ref=dst, send_sem=send, recv_sem=recv, device_id=device, device_id_type=MESH
    )
    copy.start()
    return copy


def greet(axes, others):
    barrier = pltpu.get_barrier_semaphore()
    count = 0
    for axis in axes:
        i, right, left, far = around(axis)
        for other in (right, left):
            pl.semaphore_signal(barrier, inc=1, device_id={axis: other}, device_id_type=MESH)
            count += 1
    for device in others:
        pl.semaphore_signal(barrier, inc=1, device_id=device, device_id_type=MESH)
        count += 1
    pl.semaphore_wait(barrier, count)


class Scatter:
    def __init__(self, axis, src, first, second, near, final, send, recv, add):
        self.axis, self.src, self.first, self.second = axis, src, first, second
        self.near, self.final, self.send, self.recv, self.add = near, final, send, recv, add

    def start(self):
        i, right, left, far = around(self.axis)
        src, first, second, send, recv = self.src, self.first, self.second, self.send, self.recv
        to_right, to_left = {self.axis: right}, {self.axis: left}
        self.a1 = push(first(src.at[far]), first(self.near), send.at[0], recv.at[0], to_right)
        self.b1 = push(second(src.at[far]), second(self.near), send.at[1], recv.at[1], to_left)
        self.a2 = push(second(src.at[right]), second(self.final.at[0]), send.at[2], recv.at[2], to_right)
        self.b2 = push(first(src.at[left]), first(self.final.at[1]), send.at[3], recv.at[3], to_left)

    def middle(self):
        i, right, left, far = around(self.axis)
        src, first, second, send, recv = self.src, self.first, self.second, self.send, self.recv
        self.a1.wait_recv()
        self.add(first(src.at[right]), (first(self.near),))
        self.a3 = push(first(src.at[right]), first(self.final.at[0]), send.at[4], recv.at[4], {self.axis: right})
        self.b1.wait_recv()
        self.add(second(src.at[left]), (second(self.near),))
        self.b3 = push(second(src.at[left]), second(self.final.at[1]), send.at[5], recv.at[5], {self.axis: left})

    def finish(self):
        i, right, left, far = around(self.axis)
        for copy in (self.a2, self.b2, self.a3, self.b3):
            copy.wait_recv()
        self.add(self.src.at[i], (self.final.at[0], self.final.at[1]))

    def drain(self):
        for copy in (self.a1, self.b1, self.a2, self.b2, self.a3, self.b3):
            copy.wait_send()


class Gather:
    def __init__(self, axis, buf, first, second, send, recv):
        self.axis, self.buf, self.first, self.second = axis, buf, first, second
        self.send, self.recv = send, recv

    def start(self):
        i, right, left, far = around(self.axis)
        buf = self.buf
        self.a1 = push(buf.at[i], buf.at[i], self.send.at[0], self.recv.at[0], {self.axis: right})
        self.b1 = push(buf.at[i], buf.at[i], self.send.at[1], self.recv.at[1], {self.axis: left})

    def middle(self):
        i, right, left, far = around(self.axis)
        buf, first, second = self.buf, self.first, self.second
        self.a1.wait_recv()
        self.a2 = push(first(buf.at[left]), first(buf.at[left]), self.send.at[2], self.recv.at[2], {self.axis: right})
        self.b1.wait_recv()
        self.b2 = push(second(buf.at[right]), second(buf.at[right]), self.send.at[3], self.recv.at[3], {self.axis: left})

    def finish(self):
        self.a2.wait_recv()
        self.b2.wait_recv()

    def drain(self):
        for copy in (self.a1, self.b1, self.a2, self.b2):
            copy.wait_send()


def add_blocks(dst, others):
    lead = dst.shape[:-2]
    count = 1
    for size in lead:
        count *= size

    def one(n, carry):
        index = []
        rest = n
        for size in reversed(lead):
            index.append(lax.rem(rest, size))
            rest = lax.div(rest, size)
        index = tuple(reversed(index))
        total = dst[index].astype(f32)
        for other in others:
            total = total + other[index].astype(f32)
        dst[index] = total.astype(bf16)
        return carry

    if count == 1:
        one(0, 0)
    else:
        lax.fori_loop(0, count, one, 0)


def lead_halves(size):
    half = size // 2
    return (lambda ref: ref.at[pl.ds(0, half)]), (lambda ref: ref.at[pl.ds(half, half)])


NT = (((1,), (1,)), ((), ()))


def grad_kernel(
    experts, counts, cotangent, tokens, gate, up, weight_t, out,
    mk, tk, gb, ub, gt, ut, rex, wx, wall, wfull, back_ref, left_g, left_d, *rest
):
    count = 7 * len(UNITS)
    own_sem, x_send, x_recv, w_send, w_recv, r_send, r_recv, sums, *news = rest[count:]
    pair, from_core, pair_core = news[:3]
    n_send, n_recv = news[16:18]
    y = lax.axis_index("y")
    h = lax.rem(y, 2)
    mate = y + 1 - 2 * h
    buffers = [rest[7 * k:7 * k + 7] for k in range(len(UNITS))]
    c = lax.axis_index("core")
    other = {"core": 1 - c}
    mine = pl.ds(pl.multiple_of(c * HALF, HALF), HALF)
    theirs = pl.ds(pl.multiple_of((1 - c) * HALF, HALF), HALF)
    own = []
    for n, (src, dst) in enumerate((
        (weight_t.at[:, :, mine], wx.at[c]),
        (gate.at[:, mine], gb.at[0]),
        (up.at[:, mine], ub.at[0]),
        (cotangent, mk.at[0]),
        (tokens, tk.at[0]),
    )):
        copy = pltpu.make_async_copy(src, dst, own_sem.at[n])
        copy.start()
        own.append(copy)
    lane = lax.broadcasted_iota(jnp.int32, (8, BLOCK), 1)
    for b in range(ROWS // BLOCK):
        code = jnp.where(lane < counts[b], experts[b], 2)
        rex[0, :, b * BLOCK:(b + 1) * BLOCK] = code.astype(f32)
    greet(AXES, (other, {"y": mate, "core": 1 - c}))
    cross = []
    for n, (src, dst) in enumerate((
        (weight_t.at[:, :, theirs], wx.at[c]),
        (gate.at[:, theirs], gb.at[1]),
        (up.at[:, theirs], ub.at[1]),
        (cotangent, mk.at[1]),
        (tokens, tk.at[1]),
        (rex.at[0], rex.at[1]),
    )):
        cross.append(push(src, dst, x_send.at[n], x_recv.at[n], other))

    def ready(n):
        if n < 5:
            own[n].wait()
        cross[n].wait_recv()

    z, x = lax.axis_index("z"), lax.axis_index("x")
    first, second = lead_halves(HALF)
    four_first, four_second = lead_halves(4)
    w_near = [
        Gather("z", wall.at[0, x], first, second, w_send.at[0], w_recv.at[0]),
        Gather("x", wall.at[1, z], first, second, w_send.at[1], w_recv.at[1]),
    ]
    w_far = [
        Gather("x", wall.at[0], four_first, four_second, w_send.at[2], w_recv.at[2]),
        Gather("z", wall.at[1], four_first, four_second, w_send.at[3], w_recv.at[3]),
    ]
    ready(0)
    for e in range(2):
        block = jnp.concatenate([wx[0, e], wx[1, e]], axis=0).astype(f32).T.astype(bf16)
        if e == 0:
            wall[0, x, z] = block
        else:
            wall[1, z, x] = block
    for one in w_near:
        one.start()

    rs = []
    cut = lead_halves(4)
    for k, (start, rows, order, down) in enumerate(UNITS):
        a, b = lax.axis_index(order[0]), lax.axis_index(order[1])
        part, near0, fin0, near1, fin1, near2, fin2 = buffers[k]
        rs.append(
            (
                Scatter(order[0], part, *cut, near0, fin0, r_send.at[k, 0], r_recv.at[k, 0], add_blocks),
                Scatter(order[1], part.at[a], *cut, near1, fin1, r_send.at[k, 1], r_recv.at[k, 1], add_blocks),
                Scatter(order[2], part.at[a, b], *lead_halves(rows), near2, fin2, r_send.at[k, 2], r_recv.at[k, 2], add_blocks),
            )
        )

    def make_hidden():
        for n in (1, 2, 5):
            ready(n)
        for s in range(2):
            @pl.loop(0, ROWS // BLOCK)
            def hidden_rows(t, s=s):
                rows = pl.ds(pl.multiple_of(t * BLOCK, BLOCK), BLOCK)
                there = pl.ds(pl.multiple_of(s * ROWS + t * BLOCK, BLOCK), BLOCK)
                g = gb[s, rows, :].astype(f32).T
                u = ub[s, rows, :].astype(f32).T
                gt[s, :, rows] = g.astype(bf16)
                ut[s, :, rows] = u.astype(bf16)
                hidden = g * jax.nn.sigmoid(g) * u
                which = rex[s, 0:1, rows]
                for e in range(2):
                    kept = jnp.where(which == e, hidden, 0.0).astype(bf16)
                    for h in range(2):
                        left_d[2 * e + h, :, there] = kept[h * THIRD:(h + 1) * THIRD]

    def products(picked):
        down = UNITS[picked[0]][3]
        lhs_ref, right = (left_d, mk) if down else (left_g, tk)
        low = UNITS[picked[0]][0]
        size = sum(UNITS[k][1] for k in picked)

        @pl.loop(0, 4)
        def columns(iz):
            cols = pl.ds(pl.multiple_of(iz * 512, 512), 512)
            lhs = lhs_ref[:, low:low + size, :].reshape(4 * size, 2 * ROWS)
            rhs = right[:, :, cols].reshape(2 * ROWS, 512)
            acc = jnp.dot(lhs, rhs, preferred_element_type=f32).astype(bf16)
            for k in picked:
                start, rows, order, _ = UNITS[k]
                for y in range(4):
                    first = y * size + start - low
                    for ix in range(4):
                        where = {"z": iz, "x": ix, "y": y}
                        index = tuple(where[axis] for axis in order)
                        buffers[k][0][index] = acc[first:first + rows, ix * LANES:(ix + 1) * LANES]

        for k in picked:
            rs[k][0].start()

    def pack_weights():
        for iz in range(4):
            for ix in range(4):
                cols = slice((iz * 4 + ix) * LANES, (iz * 4 + ix + 1) * LANES)
                wfull[0, :, cols] = wall[0, ix, iz]
                wfull[1, :, cols] = wall[1, iz, ix]

    def make_back(low):
        tile = 32
        for s in range(2):
            @pl.loop(0, 2)
            def back_columns(t, s=s):
                rows = pl.ds(pl.multiple_of(t * 256, 256), 256)
                lhs = wfull[:, low:low + LANES, :].reshape(2 * LANES, D)
                back_ref[:, rows] = lax.dot_general(lhs, mk[s, rows, :], NT, preferred_element_type=f32)

            @pl.loop(0, LANES // tile)
            def back_rows(t, s=s):
                rows = pl.ds(pl.multiple_of(low + t * tile, tile), tile)
                near = pl.ds(pl.multiple_of(t * tile, tile), tile)
                far = pl.ds(pl.multiple_of(LANES + t * tile, tile), tile)
                which = rex[s, 0:1, :]
                back = jnp.where(which == 0, back_ref[near, :], back_ref[far, :])
                g = gt[s, rows, :].astype(f32)
                u = ut[s, rows, :].astype(f32)
                sig = jax.nn.sigmoid(g)
                grads = (back * u * sig * (1.0 + g * (1.0 - sig)), back * g * sig)
                for e in range(2):
                    for h in range(2):
                        kept = jnp.where(which == e, grads[h], 0.0).astype(bf16)
                        left_g[2 * e + h, rows, s * ROWS:(s + 1) * ROWS] = kept

    def advance(unit, phase, what):
        if what == "m":
            rs[unit][phase].middle()
        else:
            rs[unit][phase].finish()
            if phase < 2:
                rs[unit][phase + 1].start()

    def settle(which):
        for k, (start, rows, order, down) in enumerate(UNITS):
            if down == which:
                a, b, d = (lax.axis_index(axis) for axis in order)
                start = start + (HALF if down else 0)
                sums[start:start + rows, :] = buffers[k][0][a, b, d]

    swaps = []
    for name, e, what in STEPS:
        if name == "hid":
            make_hidden()
        elif name == "pd":
            ready(3)
            products([k for k in range(len(UNITS)) if UNITS[k][3]])
        elif name == "wfull":
            pack_weights()
        elif name == "back":
            make_back(e)
        elif name == "wn":
            if what == "m":
                w_near[e].middle()
            else:
                w_near[e].finish()
                w_far[e].start()
        elif name == "wf":
            if what == "m":
                w_far[e].middle()
            else:
                w_far[e].finish()
        elif name == "prod":
            if e == 0:
                ready(4)
            products([e])
        elif name == "low":
            settle(True)
            low_rows = sums.at[pl.ds(HALF, THIRD)]
            swaps = [
                push(low_rows, pair, n_send.at[0], n_recv.at[0], {"y": mate}),
                push(low_rows, pair_core, n_send.at[2], n_recv.at[2], {"y": mate, "core": 1 - c}),
                push(low_rows, from_core.at[pl.ds(HALF, THIRD)], n_send.at[7], n_recv.at[7], other),
            ]
        else:
            advance(name, e, what)
    settle(False)
    high = pl.ds(0, HALF)
    swaps.append(push(sums.at[high], from_core.at[high], n_send.at[1], n_recv.at[1], other))
    newton_steps(swaps, c, y, h, other, out, sums, *news)
    for copy in cross:
        copy.wait_send()
    for one in w_near + w_far:
        one.drain()
    for unit in rs:
        for one in unit:
            one.drain()


def grad_update(experts, counts, cotangent, tokens, gate, up, weight_t):
    anywhere = pl.BlockSpec(memory_space=pl.ANY)
    smem = pl.BlockSpec(memory_space=pltpu.SMEM)
    vmem = pltpu.VMEM
    dma = pltpu.SemaphoreType.DMA
    square = vmem((F, F), bf16)
    buffers = []
    for start, rows, order, down in UNITS:
        block = (rows, LANES)
        for lead in ((4, 4, 4), (4, 4), (2, 4, 4), (4,), (2, 4), (), (2,)):
            buffers.append(vmem(lead + block, bf16))
    return pl.pallas_call(
        grad_kernel,
        out_shape=jax.ShapeDtypeStruct((2, 3, LANES // 2, F), bf16),
        in_specs=[smem] * 2 + [anywhere] * 5,
        out_specs=pl.BlockSpec(memory_space=vmem),
        scratch_shapes=[
            vmem((2, ROWS, D), bf16),
            vmem((2, ROWS, D), bf16),
            vmem((2, ROWS, HALF), bf16),
            vmem((2, ROWS, HALF), bf16),
            vmem((2, HALF, ROWS), bf16),
            vmem((2, HALF, ROWS), bf16),
            vmem((2, 8, ROWS), f32),
            vmem((2, 2, LANES // 2, HALF), bf16),
            vmem((2, 4, 4, HALF, LANES), bf16),
            vmem((2, HALF, D), bf16),
            vmem((2 * LANES, ROWS), f32),
            vmem((4, HALF, 2 * ROWS), bf16),
            vmem((4, THIRD, 2 * ROWS), bf16),
            *buffers,
            dma((5,)),
            dma((6,)),
            dma((6,)),
            dma((4, 4)),
            dma((4, 4)),
            dma((len(UNITS), 3, 6)),
            dma((len(UNITS), 3, 6)),
            vmem((3 * THIRD, LANES), bf16),
            vmem((THIRD, LANES), bf16),
            vmem((3 * THIRD, LANES), bf16),
            vmem((THIRD, LANES), bf16),
            vmem((4, THIRD, LANES), bf16),
            vmem((2, 4, 4, CHUNK, LANES), bf16),
            vmem((2, 4, 4, CHUNK, LANES), bf16),
            vmem((2, 4, CHUNK, LANES), bf16),
            vmem((2, 2, 4, CHUNK, LANES), bf16),
            vmem((2, 4, 4, CHUNK, LANES), bf16),
            square, square, square, square, square,
            vmem((4, LANES, F), bf16),
            vmem((4, LANES, HALF), bf16),
            dma((8,)),
            dma((8,)),
            dma((2, 2, 6)),
            dma((2, 2, 6)),
            dma((2, 2, 4)),
            dma((2, 2, 4)),
            dma((2, 4)),
            dma((2, 4)),
        ],
        compiler_params=pltpu.CompilerParams(
            collective_id=0, has_side_effects=True, vmem_limit_bytes=67043328
        ),
        name="grad_update",
    )(experts, counts, cotangent, tokens, gate, up, weight_t)


CHUNK = 96
PAIRS = ((0, 0), (0, 1), (0, 2), (1, 1), (1, 2), (2, 2))
WIDE = 256
STRIP = 32


def strips():
    for n in range(len(PAIRS) * WIDE // STRIP):
        row = n * STRIP
        yield n // 8, (n % 8) * STRIP, row // CHUNK, row % CHUNK


def newton_steps(
    swaps, c, y, h, other, out, sums,
    pair, from_core, pair_core, mat, gram, whole, near0, fin0, gath,
    g1, p1, u, g2, p2, ring0, ring1,
    x_send, x_recv, g_send, g_recv, a_send, a_recv, o_send, o_recv,
):
    for copy in swaps:
        copy.wait_recv()

    @pl.when(c == 0)
    def first_core():
        for k in range(2):
            mat[k] = sums[k * THIRD:(k + 1) * THIRD]
            mat[2 + k] = from_core[k * THIRD:(k + 1) * THIRD]

    @pl.when(c == 1)
    def second_core():
        mat[h] = from_core[HALF:]
        mat[1 - h] = pair_core[...]
        mat[2 + h] = sums[HALF:]
        mat[3 - h] = pair[...]

    X = mat[...].reshape(F, LANES)
    blocks = []
    for i, j in PAIRS:
        left, right = X[i * WIDE:(i + 1) * WIDE], X[j * WIDE:(j + 1) * WIDE]
        blocks.append(lax.dot_general(left, right, NT, preferred_element_type=f32).astype(bf16))
    for n, rows, chunk, place in strips():
        for k in range(2):
            gram[k, chunk // 4, chunk % 4, place:place + STRIP, :] = blocks[n][
                rows:rows + STRIP, k * LANES:(k + 1) * LANES
            ]

    four = lead_halves(4)
    orders = (("z", "x"), ("x", "z"))
    rs0, ag0, ag1 = [], [], []
    for k in range(2):
        first_axis, second_axis = orders[k]
        a = lax.axis_index(first_axis)
        rs0.append(Scatter(first_axis, gram.at[k], *four, near0.at[k], fin0.at[k], g_send.at[k, 0], g_recv.at[k, 0], add_blocks))
        ag0.append(Gather(second_axis, gath.at[k], *four, a_send.at[k, 0], a_recv.at[k, 0]))
        ag1.append(Gather(first_axis, whole.at[k], *four, a_send.at[k, 1], a_recv.at[k, 1]))
    for k in range(2):
        rs0[k].start()
    for k in range(2):
        rs0[k].middle()
    for k in range(2):
        rs0[k].finish()
        a, b = (lax.axis_index(axis) for axis in orders[k])
        gath[k, b] = gram[k, a]
        ag0[k].start()
    for k in range(2):
        ag0[k].middle()
    for k in range(2):
        ag0[k].finish()
        a = lax.axis_index(orders[k][0])
        for b in range(4):
            total = gath[k, 0, b].astype(f32)
            for source in range(1, 4):
                total = total + gath[k, source, b].astype(f32)
            whole[k, a, b] = total.astype(bf16)
        ag1[k].start()
    for k in range(2):
        ag1[k].middle()
    for k in range(2):
        ag1[k].finish()

    trace = jnp.zeros((STRIP, LANES), f32)
    row = lax.broadcasted_iota(jnp.int32, (STRIP, LANES), 0)
    col = lax.broadcasted_iota(jnp.int32, (STRIP, LANES), 1)
    for n, rows, chunk, place in strips():
        if PAIRS[n][0] == PAIRS[n][1]:
            k = rows // LANES
            value = whole[k, chunk // 4, chunk % 4, place:place + STRIP, :].astype(f32)
            trace = trace + jnp.where(col == row + rows % LANES, value, 0.0)
    squares = jnp.sum(jnp.sum(trace, axis=0, keepdims=True), axis=1, keepdims=True)
    scale = 1.0 / (jnp.sqrt(squares) + norm_eps)
    for n, rows, chunk, place in strips():
        i, j = PAIRS[n]
        for k in range(2):
            value = whole[k, chunk // 4, chunk % 4, place:place + STRIP, :].astype(f32) * scale * scale
            g1[i * WIDE + rows:i * WIDE + rows + STRIP, j * WIDE + k * LANES:j * WIDE + (k + 1) * LANES] = value.astype(bf16)
    for i, j in PAIRS:
        if i != j:
            block = g1[i * WIDE:(i + 1) * WIDE, j * WIDE:(j + 1) * WIDE]
            g1[j * WIDE:(j + 1) * WIDE, i * WIDE:(i + 1) * WIDE] = block.astype(f32).T.astype(bf16)

    def times(left, right, cols):
        return jnp.dot(left[...], right[:, cols], preferred_element_type=f32)

    def make_p1(cols):
        p1[:, cols] = (ns_second * g1[:, cols].astype(f32) + ns_third * times(g1, g1, cols)).astype(bf16)

    def make_u(cols):
        u[:, cols] = (ns_first * g1[:, cols].astype(f32) + times(p1, g1, cols)).astype(bf16)

    def make_g2(cols):
        g2[:, cols] = (ns_first * u[:, cols].astype(f32) + times(p1, u, cols)).astype(bf16)

    def make_p2(cols):
        p2[:, cols] = (ns_second * g2[:, cols].astype(f32) + ns_third * times(g2, g2, cols)).astype(bf16)

    for body in (make_p1, make_u, make_g2, make_p2):
        @pl.loop(0, F // WIDE)
        def one(t, body=body):
            body(pl.ds(pl.multiple_of(t * WIDE, WIDE), WIDE))

    factor = jnp.sqrt(f32(D))
    XT = X.astype(f32).T
    low = XT.astype(bf16)
    first_x = (ns_first * XT + jnp.dot(low, p1[...], preferred_element_type=f32)) * scale
    low = first_x.astype(bf16)
    i, right, left, far = around("y")
    side = LANES // 2

    @pl.when(c == 0)
    def send_first():
        new = ns_first * low.astype(f32) + jnp.dot(low, p2[...], preferred_element_type=f32)
        ring0[i] = (factor * new).astype(bf16)
        ring = Gather("y", ring0, *lead_halves(LANES), o_send.at[0], o_recv.at[0])
        place = lambda t: out.at[lax.div(t, 2), lax.rem(t, 2)]
        give = lambda t, n: push(ring0.at[t, pl.ds(side, side)], place(t), x_send.at[n], x_recv.at[n], other)
        ring.start()
        over = [give(i, 3)]
        ring.middle()
        over.append(give(left, 4))
        over.append(give(right, 5))
        ring.finish()
        over.append(give(far, 6))
        for t in range(4):
            out[t // 2, t % 2] = ring0[t, 0:side]
        for n, t in enumerate((i, left, right, far)):
            span = pl.ds(pl.multiple_of(lax.rem(t, 2) * HALF, HALF), HALF)
            expected = out.at[lax.div(t, 2), 2, :, span]
            pltpu.make_async_remote_copy(
                src_ref=expected, dst_ref=expected, send_sem=x_send.at[3 + n], recv_sem=x_recv.at[3 + n],
                device_id=other, device_id_type=MESH,
            ).wait_recv()
        for copy in over:
            copy.wait_send()
        ring.drain()

    @pl.when(c == 1)
    def send_second():
        half = pl.ds(pl.multiple_of(h * HALF, HALF), HALF)
        kept = jnp.where(h == 0, first_x[:, 0:HALF], first_x[:, HALF:])
        new = ns_first * kept.astype(bf16).astype(f32) + jnp.dot(
            low, p2[:, half], preferred_element_type=f32
        )
        ring1[i] = (factor * new).astype(bf16)
        ring = Gather("y", ring1, *lead_halves(LANES), o_send.at[1], o_recv.at[1])
        place = lambda t: out.at[lax.div(t, 2), 2, :, pl.ds(pl.multiple_of(lax.rem(t, 2) * HALF, HALF), HALF)]
        give = lambda t, n: push(ring1.at[t, pl.ds(0, side)], place(t), x_send.at[n], x_recv.at[n], other)
        ring.start()
        over = [give(i, 3)]
        ring.middle()
        over.append(give(left, 4))
        over.append(give(right, 5))
        ring.finish()
        over.append(give(far, 6))
        for t in range(4):
            out[t // 2, 2, :, (t % 2) * HALF:(t % 2 + 1) * HALF] = ring1[t, side:]
        for n, t in enumerate((i, left, right, far)):
            expected = out.at[lax.div(t, 2), lax.rem(t, 2)]
            pltpu.make_async_remote_copy(
                src_ref=expected, dst_ref=expected, send_sem=x_send.at[3 + n], recv_sem=x_recv.at[3 + n],
                device_id=other, device_id_type=MESH,
            ).wait_recv()
        for copy in over:
            copy.wait_send()
        ring.drain()

    for copy in swaps:
        copy.wait_send()
    for one in rs0 + ag0 + ag1:
        one.drain()


def per_device(
    token_inputs, cotangent, gate_preact, up_preact, down_weight, block_expert, block_count
):
    done = grad_update(
        block_expert, block_count, cotangent, token_inputs, gate_preact, up_preact,
        down_weight.swapaxes(1, 2),
    )
    return done.swapaxes(2, 3)


def solution(mesh):
    torus = Mesh(mesh.devices.reshape(4, 4, 2, mesh.shape["rep"]), ("z", "x", "core", "y"))
    dp, dp_rep = ("z", "x", "core"), ("z", "x", "core", "y")
    return jax.shard_map(
        per_device,
        mesh=torus,
        in_specs=(
            P(dp_rep, None),
            P(dp_rep, None),
            P(dp_rep, None),
            P(dp_rep, None),
            P(None, None, dp),
            P(dp_rep),
            P(dp_rep),
        ),
        out_specs=P(None, None, None, dp),
        check_vma=False,
    )
```

```python
import functools

import jax
import jax.numpy as jnp
from jax import lax
from jax.experimental import pallas as pl
from jax.experimental.pallas import tpu as pltpu
from jax.sharding import Mesh
from jax.sharding import PartitionSpec as P

D = 2048
F = 768
ROWS = 512
BLOCK = 128
HALF = F // 2
THIRD = HALF // 2
LANES = 128
AXES = ("z", "x", "y")
UNITS = (
    (0, 64, ("z", "x", "y"), False),
    (64, 64, ("x", "y", "z"), False),
    (128, 64, ("x", "y", "z"), False),
    (192, 64, ("z", "y", "x"), False),
    (256, 64, ("y", "z", "x"), False),
    (320, 32, ("z", "x", "y"), False),
    (352, 32, ("z", "x", "y"), False),
    (0, 192, ("y", "x", "z"), True),
)
STEPS = (
    ("hid", 0, ""),
    ("pd", 0, ""),
    ("wn", 0, "m"),
    ("wn", 1, "m"),
    ("pd", 1, ""),
    ("wn", 0, "f"),
    ("wn", 1, "f"),
    ("wf", 0, "m"),
    ("wf", 1, "m"),
    (7, 0, "m"),
    ("wf", 0, "f"),
    ("wf", 1, "f"),
    ("back", 0, ""),
    ("prod", 0, ""),
    ("prod", 1, ""),
    ("back", 128, ""),
    ("prod", 2, ""),
    (0, 0, "m"),
    (1, 0, "m"),
    ("prod", 3, ""),
    ("back", 256, ""),
    (0, 0, "f"),
    (7, 0, "f"),
    (2, 0, "m"),
    ("prod", 4, ""),
    (3, 0, "m"),
    ("prod", 5, ""),
    ("prod", 6, ""),
    (1, 0, "f"),
    (0, 1, "m"),
    (4, 0, "m"),
    (3, 0, "f"),
    (5, 0, "m"),
    (7, 1, "m"),
    (1, 1, "m"),
    (6, 0, "m"),
    (4, 0, "f"),
    (2, 0, "f"),
    (5, 0, "f"),
    (3, 1, "m"),
    (0, 1, "f"),
    (6, 0, "f"),
    (1, 1, "f"),
    (4, 1, "m"),
    (7, 1, "f"),
    (2, 1, "m"),
    (5, 1, "m"),
    (1, 2, "m"),
    (6, 1, "m"),
    (3, 1, "f"),
    (0, 2, "m"),
    (4, 1, "f"),
    (7, 2, "m"),
    (5, 1, "f"),
    (2, 1, "f"),
    (1, 2, "f"),
    (6, 1, "f"),
    (3, 2, "m"),
    (0, 2, "f"),
    (4, 2, "m"),
    (5, 2, "m"),
    (7, 2, "f"),
    ("low", 0, ""),
    (2, 2, "m"),
    (6, 2, "m"),
    (3, 2, "f"),
    (4, 2, "f"),
    (5, 2, "f"),
    (2, 2, "f"),
    (6, 2, "f"),
)
MESH = pl.DeviceIdType.MESH

ns_first = 3.4445
ns_second = -4.775
ns_third = 2.0315
norm_eps = 1e-07

bf16 = jnp.bfloat16
f32 = jnp.float32


def around(axis):
    i = lax.axis_index(axis)
    return i, lax.rem(i + 1, 4), lax.rem(i + 3, 4), lax.rem(i + 2, 4)


def push(src, dst, send, recv, device):
    copy = pltpu.make_async_remote_copy(
        src_ref=src, dst_ref=dst, send_sem=send, recv_sem=recv, device_id=device, device_id_type=MESH
    )
    copy.start()
    return copy


def greet(axes, others):
    barrier = pltpu.get_barrier_semaphore()
    count = 0
    for axis in axes:
        i, right, left, far = around(axis)
        for other in (right, left):
            pl.semaphore_signal(barrier, inc=1, device_id={axis: other}, device_id_type=MESH)
            count += 1
    for device in others:
        pl.semaphore_signal(barrier, inc=1, device_id=device, device_id_type=MESH)
        count += 1
    pl.semaphore_wait(barrier, count)


class Scatter:
    def __init__(self, axis, src, first, second, near, final, send, recv, add):
        self.axis, self.src, self.first, self.second = axis, src, first, second
        self.near, self.final, self.send, self.recv, self.add = near, final, send, recv, add

    def start(self):
        i, right, left, far = around(self.axis)
        src, first, second, send, recv = self.src, self.first, self.second, self.send, self.recv
        to_right, to_left = {self.axis: right}, {self.axis: left}
        self.a1 = push(first(src.at[far]), first(self.near), send.at[0], recv.at[0], to_right)
        self.b1 = push(second(src.at[far]), second(self.near), send.at[1], recv.at[1], to_left)
        self.a2 = push(second(src.at[right]), second(self.final.at[0]), send.at[2], recv.at[2], to_right)
        self.b2 = push(first(src.at[left]), first(self.final.at[1]), send.at[3], recv.at[3], to_left)

    def middle(self):
        i, right, left, far = around(self.axis)
        src, first, second, send, recv = self.src, self.first, self.second, self.send, self.recv
        self.a1.wait_recv()
        self.add(first(src.at[right]), (first(self.near),))
        self.a3 = push(first(src.at[right]), first(self.final.at[0]), send.at[4], recv.at[4], {self.axis: right})
        self.b1.wait_recv()
        self.add(second(src.at[left]), (second(self.near),))
        self.b3 = push(second(src.at[left]), second(self.final.at[1]), send.at[5], recv.at[5], {self.axis: left})

    def finish(self):
        i, right, left, far = around(self.axis)
        for copy in (self.a2, self.b2, self.a3, self.b3):
            copy.wait_recv()
        self.add(self.src.at[i], (self.final.at[0], self.final.at[1]))

    def drain(self):
        for copy in (self.a1, self.b1, self.a2, self.b2, self.a3, self.b3):
            copy.wait_send()


class Gather:
    def __init__(self, axis, buf, first, second, send, recv):
        self.axis, self.buf, self.first, self.second = axis, buf, first, second
        self.send, self.recv = send, recv

    def start(self):
        i, right, left, far = around(self.axis)
        first, second = self.first(self.buf.at[i]), self.second(self.buf.at[i])
        to_right, to_left = {self.axis: right}, {self.axis: left}
        self.a1 = push(first, first, self.send.at[0], self.recv.at[0], to_right)
        self.b1 = push(second, second, self.send.at[1], self.recv.at[1], to_left)
        self.a3 = push(second, second, self.send.at[2], self.recv.at[2], to_right)
        self.b3 = push(first, first, self.send.at[3], self.recv.at[3], to_left)

    def middle(self):
        i, right, left, far = around(self.axis)
        first, second = self.first(self.buf.at[left]), self.second(self.buf.at[right])
        self.a1.wait_recv()
        self.a2 = push(first, first, self.send.at[4], self.recv.at[4], {self.axis: right})
        self.b1.wait_recv()
        self.b2 = push(second, second, self.send.at[5], self.recv.at[5], {self.axis: left})

    def nearby(self):
        self.a3.wait_recv()
        self.b3.wait_recv()

    def finish(self):
        self.a2.wait_recv()
        self.b2.wait_recv()

    def drain(self):
        for copy in (self.a1, self.b1, self.a2, self.b2, self.a3, self.b3):
            copy.wait_send()


class Pieces:
    def __init__(self, axis, inner, buf, first, second, send, recv):
        self.axis, self.inner, self.buf, self.first, self.second = axis, inner, buf, first, second
        self.send, self.recv = send, recv
        self.rightward, self.leftward = {}, {}

    def piece(self, role):
        i, right, left, far = around(self.axis)
        src = self.buf.at[i, around(self.inner)[role]]
        self.rightward[role] = push(src, src, self.send.at[role], self.recv.at[role], {self.axis: right})
        self.leftward[role] = push(src, src, self.send.at[4 + role], self.recv.at[4 + role], {self.axis: left})

    def middle(self):
        i, right, left, far = around(self.axis)
        buf, first, second = self.buf, self.first, self.second
        for role in range(4):
            self.rightward[role].wait_recv()
        self.a2 = push(first(buf.at[left]), first(buf.at[left]), self.send.at[8], self.recv.at[8], {self.axis: right})
        for role in range(4):
            self.leftward[role].wait_recv()
        self.b2 = push(second(buf.at[right]), second(buf.at[right]), self.send.at[9], self.recv.at[9], {self.axis: left})

    def finish(self):
        self.a2.wait_recv()
        self.b2.wait_recv()

    def drain(self):
        for role in range(4):
            self.rightward[role].wait_send()
            self.leftward[role].wait_send()
        self.a2.wait_send()
        self.b2.wait_send()


def add_blocks(dst, others):
    lead = dst.shape[:-2]
    count = 1
    for size in lead:
        count *= size

    def one(n, carry):
        index = []
        rest = n
        for size in reversed(lead):
            index.append(lax.rem(rest, size))
            rest = lax.div(rest, size)
        index = tuple(reversed(index))
        total = dst[index].astype(f32)
        for other in others:
            total = total + other[index].astype(f32)
        dst[index] = total.astype(bf16)
        return carry

    if count == 1:
        one(0, 0)
    else:
        lax.fori_loop(0, count, one, 0)


def lead_halves(size):
    half = size // 2
    return (lambda ref: ref.at[pl.ds(0, half)]), (lambda ref: ref.at[pl.ds(half, half)])


NT = (((1,), (1,)), ((), ()))


def grad_kernel(
    experts, counts, cotangent, tokens, gate, up, weight_t, out,
    mk, tk, gb, ub, gt, ut, rex, wx, wall, wfull, back_ref, left_g, left_d, *rest
):
    count = 7 * len(UNITS)
    own_sem, x_send, x_recv, w_send, w_recv, r_send, r_recv, sums, *news = rest[count:]
    pair, from_core, pair_core = news[:3]
    n_send, n_recv = news[16:18]
    y = lax.axis_index("y")
    h = lax.rem(y, 2)
    mate = y + 1 - 2 * h
    buffers = [rest[7 * k:7 * k + 7] for k in range(len(UNITS))]
    c = lax.axis_index("core")
    other = {"core": 1 - c}
    mine = pl.ds(pl.multiple_of(c * HALF, HALF), HALF)
    theirs = pl.ds(pl.multiple_of((1 - c) * HALF, HALF), HALF)
    own = []
    for n, (src, dst) in enumerate((
        (weight_t.at[:, :, mine], wx.at[c]),
        (gate.at[:, mine], gb.at[0]),
        (up.at[:, mine], ub.at[0]),
        (cotangent, mk.at[0]),
        (tokens, tk.at[0]),
    )):
        copy = pltpu.make_async_copy(src, dst, own_sem.at[n])
        copy.start()
        own.append(copy)
    lane = lax.broadcasted_iota(jnp.int32, (8, BLOCK), 1)
    for b in range(ROWS // BLOCK):
        code = jnp.where(lane < counts[b], experts[b], 2)
        rex[0, :, b * BLOCK:(b + 1) * BLOCK] = code.astype(f32)
    greet(AXES, (other, {"y": mate, "core": 1 - c}))
    cross = []
    for n, (src, dst) in enumerate((
        (weight_t.at[:, :, theirs], wx.at[c]),
        (gate.at[:, theirs], gb.at[1]),
        (up.at[:, theirs], ub.at[1]),
        (cotangent, mk.at[1]),
        (tokens, tk.at[1]),
        (rex.at[0], rex.at[1]),
    )):
        cross.append(push(src, dst, x_send.at[n], x_recv.at[n], other))

    def ready(n):
        if n < 5:
            own[n].wait()
        cross[n].wait_recv()

    z, x = lax.axis_index("z"), lax.axis_index("x")
    first, second = lead_halves(HALF)
    four_first, four_second = lead_halves(4)
    w_near = [
        Gather("z", wall.at[0, x], first, second, w_send.at[0], w_recv.at[0]),
        Gather("x", wall.at[1, z], first, second, w_send.at[1], w_recv.at[1]),
    ]
    w_far = [
        Pieces("x", "z", wall.at[0], four_first, four_second, w_send.at[2], w_recv.at[2]),
        Pieces("z", "x", wall.at[1], four_first, four_second, w_send.at[3], w_recv.at[3]),
    ]
    ready(0)
    for e in range(2):
        block = jnp.concatenate([wx[0, e], wx[1, e]], axis=0).astype(f32).T.astype(bf16)
        if e == 0:
            wall[0, x, z] = block
        else:
            wall[1, z, x] = block
    for one in w_near:
        one.start()
    for one in w_far:
        one.piece(0)

    rs = []
    cut = lead_halves(4)
    for k, (start, rows, order, down) in enumerate(UNITS):
        a, b = lax.axis_index(order[0]), lax.axis_index(order[1])
        part, near0, fin0, near1, fin1, near2, fin2 = buffers[k]
        rs.append(
            (
                Scatter(order[0], part, *cut, near0, fin0, r_send.at[k, 0], r_recv.at[k, 0], add_blocks),
                Scatter(order[1], part.at[a], *cut, near1, fin1, r_send.at[k, 1], r_recv.at[k, 1], add_blocks),
                Scatter(order[2], part.at[a, b], *lead_halves(rows), near2, fin2, r_send.at[k, 2], r_recv.at[k, 2], add_blocks),
            )
        )

    def make_hidden():
        for n in (1, 2, 5):
            ready(n)
        for s in range(2):
            @pl.loop(0, ROWS // BLOCK)
            def hidden_rows(t, s=s):
                rows = pl.ds(pl.multiple_of(t * BLOCK, BLOCK), BLOCK)
                there = pl.ds(pl.multiple_of(s * ROWS + t * BLOCK, BLOCK), BLOCK)
                g = gb[s, rows, :].astype(f32).T
                u = ub[s, rows, :].astype(f32).T
                gt[s, :, rows] = g.astype(bf16)
                ut[s, :, rows] = u.astype(bf16)
                hidden = g * jax.nn.sigmoid(g) * u
                which = rex[s, 0:1, rows]
                for e in range(2):
                    kept = jnp.where(which == e, hidden, 0.0).astype(bf16)
                    for h in range(2):
                        left_d[2 * e + h, :, there] = kept[h * THIRD:(h + 1) * THIRD]

    def products(picked, begin=0, end=4):
        down = UNITS[picked[0]][3]
        lhs_ref, right = (left_d, mk) if down else (left_g, tk)
        low = UNITS[picked[0]][0]
        size = sum(UNITS[k][1] for k in picked)

        @pl.loop(begin, end)
        def columns(iz):
            cols = pl.ds(pl.multiple_of(iz * 512, 512), 512)
            lhs = lhs_ref[:, low:low + size, :].reshape(4 * size, 2 * ROWS)
            rhs = right[:, :, cols].reshape(2 * ROWS, 512)
            acc = jnp.dot(lhs, rhs, preferred_element_type=f32).astype(bf16)
            for k in picked:
                start, rows, order, _ = UNITS[k]
                for y in range(4):
                    first = y * size + start - low
                    for ix in range(4):
                        where = {"z": iz, "x": ix, "y": y}
                        index = tuple(where[axis] for axis in order)
                        buffers[k][0][index] = acc[first:first + rows, ix * LANES:(ix + 1) * LANES]

        if end == 4:
            for k in picked:
                rs[k][0].start()

    def pack_weights(rows):
        for iz in range(4):
            for ix in range(4):
                cols = slice((iz * 4 + ix) * LANES, (iz * 4 + ix + 1) * LANES)
                wfull[0, rows, cols] = wall[0, ix, iz, rows, :]
                wfull[1, rows, cols] = wall[1, iz, ix, rows, :]

    def make_back(low):
        tile = 32
        for s in range(2):
            @pl.loop(0, 2)
            def back_columns(t, s=s):
                rows = pl.ds(pl.multiple_of(t * 256, 256), 256)
                lhs = wfull[:, low:low + LANES, :].reshape(2 * LANES, D)
                back_ref[:, rows] = lax.dot_general(lhs, mk[s, rows, :], NT, preferred_element_type=f32)

            @pl.loop(0, LANES // tile)
            def back_rows(t, s=s):
                rows = pl.ds(pl.multiple_of(low + t * tile, tile), tile)
                near = pl.ds(pl.multiple_of(t * tile, tile), tile)
                far = pl.ds(pl.multiple_of(LANES + t * tile, tile), tile)
                which = rex[s, 0:1, :]
                back = jnp.where(which == 0, back_ref[near, :], back_ref[far, :])
                g = gt[s, rows, :].astype(f32)
                u = ut[s, rows, :].astype(f32)
                sig = jax.nn.sigmoid(g)
                grads = (back * u * sig * (1.0 + g * (1.0 - sig)), back * g * sig)
                for e in range(2):
                    for h in range(2):
                        kept = jnp.where(which == e, grads[h], 0.0).astype(bf16)
                        left_g[2 * e + h, rows, s * ROWS:(s + 1) * ROWS] = kept

    def advance(unit, phase, what):
        if what == "m":
            rs[unit][phase].middle()
        else:
            rs[unit][phase].finish()
            if phase < 2:
                rs[unit][phase + 1].start()

    def settle(which):
        for k, (start, rows, order, down) in enumerate(UNITS):
            if down == which:
                a, b, d = (lax.axis_index(axis) for axis in order)
                start = start + (HALF if down else 0)
                sums[start:start + rows, :] = buffers[k][0][a, b, d]

    swaps = []
    for name, e, what in STEPS:
        if name == "hid":
            make_hidden()
        elif name == "pd":
            if e == 0:
                ready(3)
            products([k for k in range(len(UNITS)) if UNITS[k][3]], 2 * e, 2 * e + 2)
        elif name == "back":
            pack_weights(slice(e, e + LANES))
            make_back(e)
        elif name == "wn":
            if what == "m":
                w_near[e].middle()
                w_near[e].nearby()
                w_far[e].piece(1)
                w_far[e].piece(2)
            else:
                w_near[e].finish()
                w_far[e].piece(3)
        elif name == "wf":
            if what == "m":
                w_far[e].middle()
            else:
                w_far[e].finish()
        elif name == "prod":
            if e == 0:
                ready(4)
            products([e])
        elif name == "low":
            settle(True)
            low_rows = sums.at[pl.ds(HALF, THIRD)]
            swaps = [
                push(low_rows, pair, n_send.at[0], n_recv.at[0], {"y": mate}),
                push(low_rows, pair_core, n_send.at[2], n_recv.at[2], {"y": mate, "core": 1 - c}),
                push(low_rows, from_core.at[pl.ds(HALF, THIRD)], n_send.at[7], n_recv.at[7], other),
            ]
        else:
            advance(name, e, what)
    settle(False)
    high = pl.ds(0, HALF)
    swaps.append(push(sums.at[high], from_core.at[high], n_send.at[1], n_recv.at[1], other))
    newton_steps(swaps, c, y, h, other, out, sums, *news)
    for copy in cross:
        copy.wait_send()
    for one in w_near + w_far:
        one.drain()
    for unit in rs:
        for one in unit:
            one.drain()


def grad_update(experts, counts, cotangent, tokens, gate, up, weight_t):
    anywhere = pl.BlockSpec(memory_space=pl.ANY)
    smem = pl.BlockSpec(memory_space=pltpu.SMEM)
    vmem = pltpu.VMEM
    dma = pltpu.SemaphoreType.DMA
    square = vmem((F, F), bf16)
    buffers = []
    for start, rows, order, down in UNITS:
        block = (rows, LANES)
        for lead in ((4, 4, 4), (4, 4), (2, 4, 4), (4,), (2, 4), (), (2,)):
            buffers.append(vmem(lead + block, bf16))
    return pl.pallas_call(
        grad_kernel,
        out_shape=jax.ShapeDtypeStruct((2, 3, LANES // 2, F), bf16),
        in_specs=[smem] * 2 + [anywhere] * 5,
        out_specs=pl.BlockSpec(memory_space=vmem),
        scratch_shapes=[
            vmem((2, ROWS, D), bf16),
            vmem((2, ROWS, D), bf16),
            vmem((2, ROWS, HALF), bf16),
            vmem((2, ROWS, HALF), bf16),
            vmem((2, HALF, ROWS), bf16),
            vmem((2, HALF, ROWS), bf16),
            vmem((2, 8, ROWS), f32),
            vmem((2, 2, LANES // 2, HALF), bf16),
            vmem((2, 4, 4, HALF, LANES), bf16),
            vmem((2, HALF, D), bf16),
            vmem((2 * LANES, ROWS), f32),
            vmem((4, HALF, 2 * ROWS), bf16),
            vmem((4, THIRD, 2 * ROWS), bf16),
            *buffers,
            dma((5,)),
            dma((6,)),
            dma((6,)),
            dma((4, 10)),
            dma((4, 10)),
            dma((len(UNITS), 3, 6)),
            dma((len(UNITS), 3, 6)),
            vmem((3 * THIRD, LANES), bf16),
            vmem((THIRD, LANES), bf16),
            vmem((3 * THIRD, LANES), bf16),
            vmem((THIRD, LANES), bf16),
            vmem((4, THIRD, LANES), bf16),
            vmem((2, 4, 4, CHUNK, LANES), bf16),
            vmem((2, 4, 4, CHUNK, LANES), bf16),
            vmem((2, 4, CHUNK, LANES), bf16),
            vmem((2, 2, 4, CHUNK, LANES), bf16),
            vmem((2, 4, 4, CHUNK, LANES), bf16),
            square, square, square, square, square,
            vmem((4, LANES, F), bf16),
            vmem((4, LANES, HALF), bf16),
            dma((8,)),
            dma((8,)),
            dma((2, 2, 6)),
            dma((2, 2, 6)),
            dma((2, 2, 6)),
            dma((2, 2, 6)),
            dma((2, 6)),
            dma((2, 6)),
        ],
        compiler_params=pltpu.CompilerParams(
            collective_id=0, has_side_effects=True, vmem_limit_bytes=67043328
        ),
        name="grad_update",
    )(experts, counts, cotangent, tokens, gate, up, weight_t)


CHUNK = 96
PAIRS = ((0, 0), (0, 1), (0, 2), (1, 1), (1, 2), (2, 2))
WIDE = 256
STRIP = 32


def strips():
    for n in range(len(PAIRS) * WIDE // STRIP):
        row = n * STRIP
        yield n // 8, (n % 8) * STRIP, row // CHUNK, row % CHUNK


def newton_steps(
    swaps, c, y, h, other, out, sums,
    pair, from_core, pair_core, mat, gram, whole, near0, fin0, gath,
    g1, p1, u, g2, p2, ring0, ring1,
    x_send, x_recv, g_send, g_recv, a_send, a_recv, o_send, o_recv,
):
    for copy in swaps:
        copy.wait_recv()

    @pl.when(c == 0)
    def first_core():
        for k in range(2):
            mat[k] = sums[k * THIRD:(k + 1) * THIRD]
            mat[2 + k] = from_core[k * THIRD:(k + 1) * THIRD]

    @pl.when(c == 1)
    def second_core():
        mat[h] = from_core[HALF:]
        mat[1 - h] = pair_core[...]
        mat[2 + h] = sums[HALF:]
        mat[3 - h] = pair[...]

    X = mat[...].reshape(F, LANES)
    blocks = []
    for i, j in PAIRS:
        left, right = X[i * WIDE:(i + 1) * WIDE], X[j * WIDE:(j + 1) * WIDE]
        blocks.append(lax.dot_general(left, right, NT, preferred_element_type=f32).astype(bf16))
    for n, rows, chunk, place in strips():
        for k in range(2):
            gram[k, chunk // 4, chunk % 4, place:place + STRIP, :] = blocks[n][
                rows:rows + STRIP, k * LANES:(k + 1) * LANES
            ]

    four = lead_halves(4)
    orders = (("z", "x"), ("x", "z"))
    rs0, ag0, ag1 = [], [], []
    for k in range(2):
        first_axis, second_axis = orders[k]
        a = lax.axis_index(first_axis)
        rs0.append(Scatter(first_axis, gram.at[k], *four, near0.at[k], fin0.at[k], g_send.at[k, 0], g_recv.at[k, 0], add_blocks))
        ag0.append(Gather(second_axis, gath.at[k], *four, a_send.at[k, 0], a_recv.at[k, 0]))
        ag1.append(Gather(first_axis, whole.at[k], *four, a_send.at[k, 1], a_recv.at[k, 1]))
    for k in range(2):
        rs0[k].start()
    for k in range(2):
        rs0[k].middle()
    for k in range(2):
        rs0[k].finish()
        a, b = (lax.axis_index(axis) for axis in orders[k])
        gath[k, b] = gram[k, a]
        ag0[k].start()
    for k in range(2):
        ag0[k].middle()
    for k in range(2):
        ag0[k].nearby()
        ag0[k].finish()
        a = lax.axis_index(orders[k][0])
        for b in range(4):
            total = gath[k, 0, b].astype(f32)
            for source in range(1, 4):
                total = total + gath[k, source, b].astype(f32)
            whole[k, a, b] = total.astype(bf16)
        ag1[k].start()
    for k in range(2):
        ag1[k].middle()
    for k in range(2):
        ag1[k].nearby()
        ag1[k].finish()

    trace = jnp.zeros((STRIP, LANES), f32)
    row = lax.broadcasted_iota(jnp.int32, (STRIP, LANES), 0)
    col = lax.broadcasted_iota(jnp.int32, (STRIP, LANES), 1)
    for n, rows, chunk, place in strips():
        if PAIRS[n][0] == PAIRS[n][1]:
            k = rows // LANES
            value = whole[k, chunk // 4, chunk % 4, place:place + STRIP, :].astype(f32)
            trace = trace + jnp.where(col == row + rows % LANES, value, 0.0)
    squares = jnp.sum(jnp.sum(trace, axis=0, keepdims=True), axis=1, keepdims=True)
    scale = 1.0 / (jnp.sqrt(squares) + norm_eps)
    for n, rows, chunk, place in strips():
        i, j = PAIRS[n]
        for k in range(2):
            value = whole[k, chunk // 4, chunk % 4, place:place + STRIP, :].astype(f32) * scale * scale
            g1[i * WIDE + rows:i * WIDE + rows + STRIP, j * WIDE + k * LANES:j * WIDE + (k + 1) * LANES] = value.astype(bf16)
    for i, j in PAIRS:
        if i != j:
            block = g1[i * WIDE:(i + 1) * WIDE, j * WIDE:(j + 1) * WIDE]
            g1[j * WIDE:(j + 1) * WIDE, i * WIDE:(i + 1) * WIDE] = block.astype(f32).T.astype(bf16)

    def times(left, right, cols):
        return jnp.dot(left[...], right[:, cols], preferred_element_type=f32)

    def make_p1(cols):
        p1[:, cols] = (ns_second * g1[:, cols].astype(f32) + ns_third * times(g1, g1, cols)).astype(bf16)

    def make_u(cols):
        u[:, cols] = (ns_first * g1[:, cols].astype(f32) + times(p1, g1, cols)).astype(bf16)

    def make_g2(cols):
        g2[:, cols] = (ns_first * u[:, cols].astype(f32) + times(p1, u, cols)).astype(bf16)

    def make_p2(cols):
        p2[:, cols] = (ns_second * g2[:, cols].astype(f32) + ns_third * times(g2, g2, cols)).astype(bf16)

    for body in (make_p1, make_u, make_g2, make_p2):
        @pl.loop(0, F // WIDE)
        def one(t, body=body):
            body(pl.ds(pl.multiple_of(t * WIDE, WIDE), WIDE))

    factor = jnp.sqrt(f32(D))
    XT = X.astype(f32).T
    low = XT.astype(bf16)
    first_x = (ns_first * XT + jnp.dot(low, p1[...], preferred_element_type=f32)) * scale
    low = first_x.astype(bf16)
    i, right, left, far = around("y")
    side = LANES // 2

    @pl.when(c == 0)
    def send_first():
        new = ns_first * low.astype(f32) + jnp.dot(low, p2[...], preferred_element_type=f32)
        ring0[i] = (factor * new).astype(bf16)
        ring = Gather("y", ring0, *lead_halves(LANES), o_send.at[0], o_recv.at[0])
        place = lambda t: out.at[lax.div(t, 2), lax.rem(t, 2)]
        give = lambda t, n: push(ring0.at[t, pl.ds(side, side)], place(t), x_send.at[n], x_recv.at[n], other)
        ring.start()
        over = [give(i, 3)]
        ring.middle()
        ring.nearby()
        over.append(give(left, 4))
        over.append(give(right, 5))
        ring.finish()
        over.append(give(far, 6))
        for t in range(4):
            out[t // 2, t % 2] = ring0[t, 0:side]
        for n, t in enumerate((i, left, right, far)):
            span = pl.ds(pl.multiple_of(lax.rem(t, 2) * HALF, HALF), HALF)
            expected = out.at[lax.div(t, 2), 2, :, span]
            pltpu.make_async_remote_copy(
                src_ref=expected, dst_ref=expected, send_sem=x_send.at[3 + n], recv_sem=x_recv.at[3 + n],
                device_id=other, device_id_type=MESH,
            ).wait_recv()
        for copy in over:
            copy.wait_send()
        ring.drain()

    @pl.when(c == 1)
    def send_second():
        half = pl.ds(pl.multiple_of(h * HALF, HALF), HALF)
        kept = jnp.where(h == 0, first_x[:, 0:HALF], first_x[:, HALF:])
        new = ns_first * kept.astype(bf16).astype(f32) + jnp.dot(
            low, p2[:, half], preferred_element_type=f32
        )
        ring1[i] = (factor * new).astype(bf16)
        ring = Gather("y", ring1, *lead_halves(LANES), o_send.at[1], o_recv.at[1])
        place = lambda t: out.at[lax.div(t, 2), 2, :, pl.ds(pl.multiple_of(lax.rem(t, 2) * HALF, HALF), HALF)]
        give = lambda t, n: push(ring1.at[t, pl.ds(0, side)], place(t), x_send.at[n], x_recv.at[n], other)
        ring.start()
        over = [give(i, 3)]
        ring.middle()
        ring.nearby()
        over.append(give(left, 4))
        over.append(give(right, 5))
        ring.finish()
        over.append(give(far, 6))
        for t in range(4):
            out[t // 2, 2, :, (t % 2) * HALF:(t % 2 + 1) * HALF] = ring1[t, side:]
        for n, t in enumerate((i, left, right, far)):
            expected = out.at[lax.div(t, 2), lax.rem(t, 2)]
            pltpu.make_async_remote_copy(
                src_ref=expected, dst_ref=expected, send_sem=x_send.at[3 + n], recv_sem=x_recv.at[3 + n],
                device_id=other, device_id_type=MESH,
            ).wait_recv()
        for copy in over:
            copy.wait_send()
        ring.drain()

    for copy in swaps:
        copy.wait_send()
    for one in rs0 + ag0 + ag1:
        one.drain()


def per_device(
    token_inputs, cotangent, gate_preact, up_preact, down_weight, block_expert, block_count
):
    done = grad_update(
        block_expert, block_count, cotangent, token_inputs, gate_preact, up_preact,
        down_weight.swapaxes(1, 2),
    )
    return done.swapaxes(2, 3)


def solution(mesh):
    torus = Mesh(mesh.devices.reshape(4, 4, 2, mesh.shape["rep"]), ("z", "x", "core", "y"))
    dp, dp_rep = ("z", "x", "core"), ("z", "x", "core", "y")
    return jax.shard_map(
        per_device,
        mesh=torus,
        in_specs=(
            P(dp_rep, None),
            P(dp_rep, None),
            P(dp_rep, None),
            P(dp_rep, None),
            P(None, None, dp),
            P(dp_rep),
            P(dp_rep),
        ),
        out_specs=P(None, None, None, dp),
        check_vma=False,
    )
```

```python
import jax
import jax.numpy as jnp
from jax import lax
from jax.experimental import pallas as pl
from jax.experimental.pallas import tpu as pltpu
from jax.sharding import Mesh
from jax.sharding import PartitionSpec as P

D = 2048
F = 768
ROWS = 512
BLOCK = 128
HALF = F // 2
THIRD = HALF // 2
LANES = 128
AXES = ("z", "x", "y")
UNITS = (
    (0, 64, ("z", "x", "y"), False),
    (64, 64, ("x", "y", "z"), False),
    (128, 64, ("x", "y", "z"), False),
    (192, 64, ("z", "y", "x"), False),
    (256, 64, ("y", "z", "x"), False),
    (320, 32, ("z", "x", "y"), False),
    (352, 32, ("z", "x", "y"), False),
    (0, 192, ("y", "x", "z"), True),
)
STEPS = (
    ("hid", 0, ""),
    ("pd", 0, ""),
    ("wn", 0, "m"),
    ("wn", 1, "m"),
    ("pd", 1, ""),
    ("wn", 0, "f"),
    ("wn", 1, "f"),
    ("wf", 0, "m"),
    ("wf", 1, "m"),
    (7, 0, "m"),
    ("wf", 0, "f"),
    ("wf", 1, "f"),
    ("back", 0, ""),
    ("prod", 0, ""),
    ("prod", 1, ""),
    ("back", 128, ""),
    ("prod", 2, ""),
    (0, 0, "m"),
    (1, 0, "m"),
    ("prod", 3, ""),
    ("back", 256, ""),
    (0, 0, "f"),
    (7, 0, "f"),
    (2, 0, "m"),
    ("prod", 4, ""),
    (3, 0, "m"),
    ("prod", 5, ""),
    ("prod", 6, ""),
    (1, 0, "f"),
    (0, 1, "m"),
    (4, 0, "m"),
    (3, 0, "f"),
    (5, 0, "m"),
    (7, 1, "m"),
    (1, 1, "m"),
    (6, 0, "m"),
    (4, 0, "f"),
    (2, 0, "f"),
    (5, 0, "f"),
    (3, 1, "m"),
    (0, 1, "f"),
    (6, 0, "f"),
    (1, 1, "f"),
    (4, 1, "m"),
    (7, 1, "f"),
    (2, 1, "m"),
    (5, 1, "m"),
    (1, 2, "m"),
    (6, 1, "m"),
    (3, 1, "f"),
    (0, 2, "m"),
    (4, 1, "f"),
    (7, 2, "m"),
    (5, 1, "f"),
    (2, 1, "f"),
    (1, 2, "f"),
    (6, 1, "f"),
    (3, 2, "m"),
    (0, 2, "f"),
    (4, 2, "m"),
    (5, 2, "m"),
    (7, 2, "f"),
    ("low", 0, ""),
    (2, 2, "m"),
    (6, 2, "m"),
    (3, 2, "f"),
    (4, 2, "f"),
    (5, 2, "f"),
    (2, 2, "f"),
    (6, 2, "f"),
)
MESH = pl.DeviceIdType.MESH

ns_first = 3.4445
ns_second = -4.775
ns_third = 2.0315
norm_eps = 1e-07

bf16 = jnp.bfloat16
f32 = jnp.float32


def around(axis):
    i = lax.axis_index(axis)
    return i, lax.rem(i + 1, 4), lax.rem(i + 3, 4), lax.rem(i + 2, 4)


def push(src, dst, send, recv, device):
    copy = pltpu.make_async_remote_copy(
        src_ref=src, dst_ref=dst, send_sem=send, recv_sem=recv, device_id=device, device_id_type=MESH
    )
    copy.start()
    return copy


def greet(axes, others):
    barrier = pltpu.get_barrier_semaphore()
    count = 0
    for axis in axes:
        i, right, left, far = around(axis)
        for other in (right, left):
            pl.semaphore_signal(barrier, inc=1, device_id={axis: other}, device_id_type=MESH)
            count += 1
    for device in others:
        pl.semaphore_signal(barrier, inc=1, device_id=device, device_id_type=MESH)
        count += 1
    pl.semaphore_wait(barrier, count)


class Scatter:
    def __init__(self, axis, src, first, second, near, final, send, recv, add):
        self.axis, self.src, self.first, self.second = axis, src, first, second
        self.near, self.final, self.send, self.recv, self.add = near, final, send, recv, add

    def start(self):
        i, right, left, far = around(self.axis)
        src, first, second, send, recv = self.src, self.first, self.second, self.send, self.recv
        to_right, to_left = {self.axis: right}, {self.axis: left}
        self.a1 = push(first(src.at[far]), first(self.near), send.at[0], recv.at[0], to_right)
        self.b1 = push(second(src.at[far]), second(self.near), send.at[1], recv.at[1], to_left)
        self.a2 = push(second(src.at[right]), second(self.final.at[0]), send.at[2], recv.at[2], to_right)
        self.b2 = push(first(src.at[left]), first(self.final.at[1]), send.at[3], recv.at[3], to_left)

    def middle(self):
        i, right, left, far = around(self.axis)
        src, first, second, send, recv = self.src, self.first, self.second, self.send, self.recv
        self.a1.wait_recv()
        self.add(first(src.at[right]), (first(self.near),))
        self.a3 = push(first(src.at[right]), first(self.final.at[0]), send.at[4], recv.at[4], {self.axis: right})
        self.b1.wait_recv()
        self.add(second(src.at[left]), (second(self.near),))
        self.b3 = push(second(src.at[left]), second(self.final.at[1]), send.at[5], recv.at[5], {self.axis: left})

    def finish(self):
        i, right, left, far = around(self.axis)
        for copy in (self.a2, self.b2, self.a3, self.b3):
            copy.wait_recv()
        self.add(self.src.at[i], (self.final.at[0], self.final.at[1]))

    def drain(self):
        for copy in (self.a1, self.b1, self.a2, self.b2, self.a3, self.b3):
            copy.wait_send()


class Gather:
    def __init__(self, axis, buf, first, second, send, recv):
        self.axis, self.buf, self.first, self.second = axis, buf, first, second
        self.send, self.recv = send, recv

    def start(self):
        i, right, left, far = around(self.axis)
        first, second = self.first(self.buf.at[i]), self.second(self.buf.at[i])
        to_right, to_left = {self.axis: right}, {self.axis: left}
        self.a1 = push(first, first, self.send.at[0], self.recv.at[0], to_right)
        self.b1 = push(second, second, self.send.at[1], self.recv.at[1], to_left)
        self.a3 = push(second, second, self.send.at[2], self.recv.at[2], to_right)
        self.b3 = push(first, first, self.send.at[3], self.recv.at[3], to_left)

    def middle(self):
        i, right, left, far = around(self.axis)
        first, second = self.first(self.buf.at[left]), self.second(self.buf.at[right])
        self.a1.wait_recv()
        self.a2 = push(first, first, self.send.at[4], self.recv.at[4], {self.axis: right})
        self.b1.wait_recv()
        self.b2 = push(second, second, self.send.at[5], self.recv.at[5], {self.axis: left})

    def nearby(self):
        self.a3.wait_recv()
        self.b3.wait_recv()

    def finish(self):
        self.a2.wait_recv()
        self.b2.wait_recv()

    def drain(self):
        for copy in (self.a1, self.b1, self.a2, self.b2, self.a3, self.b3):
            copy.wait_send()


class Pieces:
    def __init__(self, axis, inner, buf, first, second, send, recv):
        self.axis, self.inner, self.buf, self.first, self.second = axis, inner, buf, first, second
        self.send, self.recv = send, recv
        self.rightward, self.leftward = {}, {}

    def piece(self, role):
        i, right, left, far = around(self.axis)
        src = self.buf.at[i, around(self.inner)[role]]
        self.rightward[role] = push(src, src, self.send.at[role], self.recv.at[role], {self.axis: right})
        self.leftward[role] = push(src, src, self.send.at[4 + role], self.recv.at[4 + role], {self.axis: left})

    def forward(self, role):
        i, right, left, far = around(self.axis)
        place = around(self.inner)[role]
        first, second = self.first(self.buf.at[left, place]), self.second(self.buf.at[right, place])
        self.rightward[role].wait_recv()
        self.rightward[8 + role] = push(
            first, first, self.send.at[8 + role], self.recv.at[8 + role], {self.axis: right}
        )
        self.leftward[role].wait_recv()
        self.leftward[8 + role] = push(
            second, second, self.send.at[12 + role], self.recv.at[12 + role], {self.axis: left}
        )

    def finish(self):
        for role in range(8, 12):
            self.rightward[role].wait_recv()
            self.leftward[role].wait_recv()

    def drain(self):
        for role in self.rightward:
            self.rightward[role].wait_send()
            self.leftward[role].wait_send()


def add_blocks(dst, others):
    lead = dst.shape[:-2]
    count = 1
    for size in lead:
        count *= size

    def one(n, carry):
        index = []
        rest = n
        for size in reversed(lead):
            index.append(lax.rem(rest, size))
            rest = lax.div(rest, size)
        index = tuple(reversed(index))
        total = dst[index].astype(f32)
        for other in others:
            total = total + other[index].astype(f32)
        dst[index] = total.astype(bf16)
        return carry

    if count == 1:
        one(0, 0)
    else:
        lax.fori_loop(0, count, one, 0)


def lead_halves(size):
    half = size // 2
    return (lambda ref: ref.at[pl.ds(0, half)]), (lambda ref: ref.at[pl.ds(half, half)])


NT = (((1,), (1,)), ((), ()))


def grad_kernel(
    experts, counts, cotangent, tokens, gate, up, weight_t, out,
    mk, tk, gb, ub, gt, ut, rex, wx, wall, wfull, back_ref, left_g, left_d, *rest
):
    count = 7 * len(UNITS)
    own_sem, x_send, x_recv, w_send, w_recv, r_send, r_recv, sums, *news = rest[count:]
    pair, from_core, pair_core = news[:3]
    n_send, n_recv = news[16:18]
    y = lax.axis_index("y")
    h = lax.rem(y, 2)
    mate = y + 1 - 2 * h
    buffers = [rest[7 * k:7 * k + 7] for k in range(len(UNITS))]
    c = lax.axis_index("core")
    other = {"core": 1 - c}
    mine = pl.ds(pl.multiple_of(c * HALF, HALF), HALF)
    theirs = pl.ds(pl.multiple_of((1 - c) * HALF, HALF), HALF)
    own = []
    for n, (src, dst) in enumerate((
        (weight_t.at[:, :, mine], wx.at[c]),
        (gate.at[:, mine], gb.at[0]),
        (up.at[:, mine], ub.at[0]),
        (cotangent, mk.at[0]),
        (tokens, tk.at[0]),
    )):
        copy = pltpu.make_async_copy(src, dst, own_sem.at[n])
        copy.start()
        own.append(copy)
    lane = lax.broadcasted_iota(jnp.int32, (8, BLOCK), 1)
    for b in range(ROWS // BLOCK):
        code = jnp.where(lane < counts[b], experts[b], 2)
        rex[0, :, b * BLOCK:(b + 1) * BLOCK] = code.astype(f32)
    greet(AXES, (other, {"y": mate, "core": 1 - c}))
    cross = []
    for n, (src, dst) in enumerate((
        (weight_t.at[:, :, theirs], wx.at[c]),
        (gate.at[:, theirs], gb.at[1]),
        (up.at[:, theirs], ub.at[1]),
        (cotangent, mk.at[1]),
        (tokens, tk.at[1]),
        (rex.at[0], rex.at[1]),
    )):
        cross.append(push(src, dst, x_send.at[n], x_recv.at[n], other))

    def ready(n):
        if n < 5:
            own[n].wait()
        cross[n].wait_recv()

    z, x = lax.axis_index("z"), lax.axis_index("x")
    first, second = lead_halves(HALF)
    w_near = [
        Gather("z", wall.at[0, x], first, second, w_send.at[0], w_recv.at[0]),
        Gather("x", wall.at[1, z], first, second, w_send.at[1], w_recv.at[1]),
    ]
    w_far = [
        Pieces("x", "z", wall.at[0], first, second, w_send.at[2], w_recv.at[2]),
        Pieces("z", "x", wall.at[1], first, second, w_send.at[3], w_recv.at[3]),
    ]
    ready(0)
    for e in range(2):
        block = jnp.concatenate([wx[0, e], wx[1, e]], axis=0).astype(f32).T.astype(bf16)
        if e == 0:
            wall[0, x, z] = block
        else:
            wall[1, z, x] = block
    for one in w_near:
        one.start()
    for one in w_far:
        one.piece(0)

    rs = []
    cut = lead_halves(4)
    for k, (start, rows, order, down) in enumerate(UNITS):
        a, b = lax.axis_index(order[0]), lax.axis_index(order[1])
        part, near0, fin0, near1, fin1, near2, fin2 = buffers[k]
        rs.append(
            (
                Scatter(order[0], part, *cut, near0, fin0, r_send.at[k, 0], r_recv.at[k, 0], add_blocks),
                Scatter(order[1], part.at[a], *cut, near1, fin1, r_send.at[k, 1], r_recv.at[k, 1], add_blocks),
                Scatter(order[2], part.at[a, b], *lead_halves(rows), near2, fin2, r_send.at[k, 2], r_recv.at[k, 2], add_blocks),
            )
        )

    def make_hidden():
        for n in (1, 2, 5):
            ready(n)
        for s in range(2):
            @pl.loop(0, ROWS // BLOCK)
            def hidden_rows(t, s=s):
                rows = pl.ds(pl.multiple_of(t * BLOCK, BLOCK), BLOCK)
                there = pl.ds(pl.multiple_of(s * ROWS + t * BLOCK, BLOCK), BLOCK)
                g = gb[s, rows, :].astype(f32).T
                u = ub[s, rows, :].astype(f32).T
                gt[s, :, rows] = g.astype(bf16)
                ut[s, :, rows] = u.astype(bf16)
                hidden = g * jax.nn.sigmoid(g) * u
                which = rex[s, 0:1, rows]
                for e in range(2):
                    kept = jnp.where(which == e, hidden, 0.0).astype(bf16)
                    for h in range(2):
                        left_d[2 * e + h, :, there] = kept[h * THIRD:(h + 1) * THIRD]

    def products(picked, begin=0, end=4):
        down = UNITS[picked[0]][3]
        lhs_ref, right = (left_d, mk) if down else (left_g, tk)
        low = UNITS[picked[0]][0]
        size = sum(UNITS[k][1] for k in picked)

        @pl.loop(begin, end)
        def columns(iz):
            cols = pl.ds(pl.multiple_of(iz * 512, 512), 512)
            lhs = lhs_ref[:, low:low + size, :].reshape(4 * size, 2 * ROWS)
            rhs = right[:, :, cols].reshape(2 * ROWS, 512)
            acc = jnp.dot(lhs, rhs, preferred_element_type=f32).astype(bf16)
            for k in picked:
                start, rows, order, _ = UNITS[k]
                for y in range(4):
                    first = y * size + start - low
                    for ix in range(4):
                        where = {"z": iz, "x": ix, "y": y}
                        index = tuple(where[axis] for axis in order)
                        buffers[k][0][index] = acc[first:first + rows, ix * LANES:(ix + 1) * LANES]

        if end == 4:
            for k in picked:
                rs[k][0].start()

    def pack_weights(rows):
        for iz in range(4):
            for ix in range(4):
                cols = slice((iz * 4 + ix) * LANES, (iz * 4 + ix + 1) * LANES)
                wfull[0, rows, cols] = wall[0, ix, iz, rows, :]
                wfull[1, rows, cols] = wall[1, iz, ix, rows, :]

    def make_back(low):
        tile = 32
        for s in range(2):
            @pl.loop(0, 2)
            def back_columns(t, s=s):
                rows = pl.ds(pl.multiple_of(t * 256, 256), 256)
                lhs = wfull[:, low:low + LANES, :].reshape(2 * LANES, D)
                back_ref[:, rows] = lax.dot_general(lhs, mk[s, rows, :], NT, preferred_element_type=f32)

            @pl.loop(0, LANES // tile)
            def back_rows(t, s=s):
                rows = pl.ds(pl.multiple_of(low + t * tile, tile), tile)
                near = pl.ds(pl.multiple_of(t * tile, tile), tile)
                far = pl.ds(pl.multiple_of(LANES + t * tile, tile), tile)
                which = rex[s, 0:1, :]
                back = jnp.where(which == 0, back_ref[near, :], back_ref[far, :])
                g = gt[s, rows, :].astype(f32)
                u = ut[s, rows, :].astype(f32)
                sig = jax.nn.sigmoid(g)
                grads = (back * u * sig * (1.0 + g * (1.0 - sig)), back * g * sig)
                for e in range(2):
                    for h in range(2):
                        kept = jnp.where(which == e, grads[h], 0.0).astype(bf16)
                        left_g[2 * e + h, rows, s * ROWS:(s + 1) * ROWS] = kept

    def advance(unit, phase, what):
        if what == "m":
            rs[unit][phase].middle()
        else:
            rs[unit][phase].finish()
            if phase < 2:
                rs[unit][phase + 1].start()

    def settle(which):
        for k, (start, rows, order, down) in enumerate(UNITS):
            if down == which:
                a, b, d = (lax.axis_index(axis) for axis in order)
                start = start + (HALF if down else 0)
                sums[start:start + rows, :] = buffers[k][0][a, b, d]

    swaps = []
    for name, e, what in STEPS:
        if name == "hid":
            make_hidden()
        elif name == "pd":
            if e == 0:
                ready(3)
            products([k for k in range(len(UNITS)) if UNITS[k][3]], 2 * e, 2 * e + 2)
        elif name == "back":
            pack_weights(slice(e, e + LANES))
            make_back(e)
        elif name == "wn":
            if what == "m":
                w_near[e].middle()
                w_near[e].nearby()
                w_far[e].piece(1)
                w_far[e].piece(2)
            else:
                w_near[e].finish()
                w_far[e].piece(3)
                w_far[e].forward(0)
        elif name == "wf":
            if what == "m":
                for role in (1, 2, 3):
                    w_far[e].forward(role)
            else:
                w_far[e].finish()
        elif name == "prod":
            if e == 0:
                ready(4)
            products([e])
        elif name == "low":
            settle(True)
            low_rows = sums.at[pl.ds(HALF, THIRD)]
            swaps = [
                push(low_rows, pair, n_send.at[0], n_recv.at[0], {"y": mate}),
                push(low_rows, pair_core, n_send.at[2], n_recv.at[2], {"y": mate, "core": 1 - c}),
                push(low_rows, from_core.at[pl.ds(HALF, THIRD)], n_send.at[7], n_recv.at[7], other),
            ]
        else:
            advance(name, e, what)
    settle(False)
    high = pl.ds(0, HALF)
    swaps.append(push(sums.at[high], from_core.at[high], n_send.at[1], n_recv.at[1], other))
    newton_steps(swaps, c, y, h, other, out, sums, *news)
    for copy in cross:
        copy.wait_send()
    for one in w_near + w_far:
        one.drain()
    for unit in rs:
        for one in unit:
            one.drain()


def grad_update(experts, counts, cotangent, tokens, gate, up, weight_t):
    anywhere = pl.BlockSpec(memory_space=pl.ANY)
    smem = pl.BlockSpec(memory_space=pltpu.SMEM)
    vmem = pltpu.VMEM
    dma = pltpu.SemaphoreType.DMA
    square = vmem((F, F), bf16)
    buffers = []
    for start, rows, order, down in UNITS:
        block = (rows, LANES)
        for lead in ((4, 4, 4), (4, 4), (2, 4, 4), (4,), (2, 4), (), (2,)):
            buffers.append(vmem(lead + block, bf16))
    return pl.pallas_call(
        grad_kernel,
        out_shape=jax.ShapeDtypeStruct((2, 3, LANES // 2, F), bf16),
        in_specs=[smem] * 2 + [anywhere] * 5,
        out_specs=pl.BlockSpec(memory_space=vmem),
        scratch_shapes=[
            vmem((2, ROWS, D), bf16),
            vmem((2, ROWS, D), bf16),
            vmem((2, ROWS, HALF), bf16),
            vmem((2, ROWS, HALF), bf16),
            vmem((2, HALF, ROWS), bf16),
            vmem((2, HALF, ROWS), bf16),
            vmem((2, 8, ROWS), f32),
            vmem((2, 2, LANES // 2, HALF), bf16),
            vmem((2, 4, 4, HALF, LANES), bf16),
            vmem((2, HALF, D), bf16),
            vmem((2 * LANES, ROWS), f32),
            vmem((4, HALF, 2 * ROWS), bf16),
            vmem((4, THIRD, 2 * ROWS), bf16),
            *buffers,
            dma((5,)),
            dma((6,)),
            dma((6,)),
            dma((4, 16)),
            dma((4, 16)),
            dma((len(UNITS), 3, 6)),
            dma((len(UNITS), 3, 6)),
            vmem((3 * THIRD, LANES), bf16),
            vmem((THIRD, LANES), bf16),
            vmem((3 * THIRD, LANES), bf16),
            vmem((THIRD, LANES), bf16),
            vmem((4, THIRD, LANES), bf16),
            vmem((2, 4, 4, CHUNK, LANES), bf16),
            vmem((2, 4, 4, CHUNK, LANES), bf16),
            vmem((2, 4, CHUNK, LANES), bf16),
            vmem((2, 2, 4, CHUNK, LANES), bf16),
            vmem((2, 4, 4, CHUNK, LANES), bf16),
            square, square, square, square, square,
            vmem((4, LANES, F), bf16),
            vmem((4, LANES, HALF), bf16),
            dma((8,)),
            dma((8,)),
            dma((2, 2, 6)),
            dma((2, 2, 6)),
            dma((2, 2, 6)),
            dma((2, 2, 6)),
            dma((2, 6)),
            dma((2, 6)),
        ],
        compiler_params=pltpu.CompilerParams(
            collective_id=0, has_side_effects=True, vmem_limit_bytes=67043328
        ),
        name="grad_update",
    )(experts, counts, cotangent, tokens, gate, up, weight_t)


CHUNK = 96
PAIRS = ((0, 0), (0, 1), (0, 2), (1, 1), (1, 2), (2, 2))
WIDE = 256
STRIP = 32


def strips():
    for n in range(len(PAIRS) * WIDE // STRIP):
        row = n * STRIP
        yield n // 8, (n % 8) * STRIP, row // CHUNK, row % CHUNK


def newton_steps(
    swaps, c, y, h, other, out, sums,
    pair, from_core, pair_core, mat, gram, whole, near0, fin0, gath,
    g1, p1, u, g2, p2, ring0, ring1,
    x_send, x_recv, g_send, g_recv, a_send, a_recv, o_send, o_recv,
):
    for copy in swaps:
        copy.wait_recv()

    @pl.when(c == 0)
    def first_core():
        for k in range(2):
            mat[k] = sums[k * THIRD:(k + 1) * THIRD]
            mat[2 + k] = from_core[k * THIRD:(k + 1) * THIRD]

    @pl.when(c == 1)
    def second_core():
        mat[h] = from_core[HALF:]
        mat[1 - h] = pair_core[...]
        mat[2 + h] = sums[HALF:]
        mat[3 - h] = pair[...]

    X = mat[...].reshape(F, LANES)
    blocks = []
    for i, j in PAIRS:
        left, right = X[i * WIDE:(i + 1) * WIDE], X[j * WIDE:(j + 1) * WIDE]
        blocks.append(lax.dot_general(left, right, NT, preferred_element_type=f32).astype(bf16))
    for n, rows, chunk, place in strips():
        for k in range(2):
            gram[k, chunk // 4, chunk % 4, place:place + STRIP, :] = blocks[n][
                rows:rows + STRIP, k * LANES:(k + 1) * LANES
            ]

    four = lead_halves(4)
    orders = (("z", "x"), ("x", "z"))
    rs0, ag0, ag1 = [], [], []
    for k in range(2):
        first_axis, second_axis = orders[k]
        a = lax.axis_index(first_axis)
        rs0.append(Scatter(first_axis, gram.at[k], *four, near0.at[k], fin0.at[k], g_send.at[k, 0], g_recv.at[k, 0], add_blocks))
        ag0.append(Gather(second_axis, gath.at[k], *four, a_send.at[k, 0], a_recv.at[k, 0]))
        ag1.append(Gather(first_axis, whole.at[k], *four, a_send.at[k, 1], a_recv.at[k, 1]))
    for k in range(2):
        rs0[k].start()
    for k in range(2):
        rs0[k].middle()
    for k in range(2):
        rs0[k].finish()
        a, b = (lax.axis_index(axis) for axis in orders[k])
        gath[k, b] = gram[k, a]
        ag0[k].start()
    for k in range(2):
        ag0[k].middle()
    for k in range(2):
        ag0[k].nearby()
        ag0[k].finish()
        a = lax.axis_index(orders[k][0])
        for b in range(4):
            total = gath[k, 0, b].astype(f32)
            for source in range(1, 4):
                total = total + gath[k, source, b].astype(f32)
            whole[k, a, b] = total.astype(bf16)
        ag1[k].start()
    for k in range(2):
        ag1[k].middle()
    for k in range(2):
        ag1[k].nearby()
        ag1[k].finish()

    trace = jnp.zeros((STRIP, LANES), f32)
    row = lax.broadcasted_iota(jnp.int32, (STRIP, LANES), 0)
    col = lax.broadcasted_iota(jnp.int32, (STRIP, LANES), 1)
    for n, rows, chunk, place in strips():
        if PAIRS[n][0] == PAIRS[n][1]:
            k = rows // LANES
            value = whole[k, chunk // 4, chunk % 4, place:place + STRIP, :].astype(f32)
            trace = trace + jnp.where(col == row + rows % LANES, value, 0.0)
    squares = jnp.sum(jnp.sum(trace, axis=0, keepdims=True), axis=1, keepdims=True)
    scale = 1.0 / (jnp.sqrt(squares) + norm_eps)
    for n, rows, chunk, place in strips():
        i, j = PAIRS[n]
        for k in range(2):
            value = whole[k, chunk // 4, chunk % 4, place:place + STRIP, :].astype(f32) * scale * scale
            g1[i * WIDE + rows:i * WIDE + rows + STRIP, j * WIDE + k * LANES:j * WIDE + (k + 1) * LANES] = value.astype(bf16)
    for i, j in PAIRS:
        if i != j:
            block = g1[i * WIDE:(i + 1) * WIDE, j * WIDE:(j + 1) * WIDE]
            g1[j * WIDE:(j + 1) * WIDE, i * WIDE:(i + 1) * WIDE] = block.astype(f32).T.astype(bf16)

    def times(left, right, cols):
        return jnp.dot(left[...], right[:, cols], preferred_element_type=f32)

    def make_p1(cols):
        p1[:, cols] = (ns_second * g1[:, cols].astype(f32) + ns_third * times(g1, g1, cols)).astype(bf16)

    def make_u(cols):
        u[:, cols] = (ns_first * g1[:, cols].astype(f32) + times(p1, g1, cols)).astype(bf16)

    def make_g2(cols):
        g2[:, cols] = (ns_first * u[:, cols].astype(f32) + times(p1, u, cols)).astype(bf16)

    def make_p2(cols):
        p2[:, cols] = (ns_second * g2[:, cols].astype(f32) + ns_third * times(g2, g2, cols)).astype(bf16)

    for body in (make_p1, make_u, make_g2, make_p2):
        @pl.loop(0, F // WIDE)
        def one(t, body=body):
            body(pl.ds(pl.multiple_of(t * WIDE, WIDE), WIDE))

    factor = jnp.sqrt(f32(D))
    XT = X.astype(f32).T
    low = XT.astype(bf16)
    first_x = (ns_first * XT + jnp.dot(low, p1[...], preferred_element_type=f32)) * scale
    low = first_x.astype(bf16)
    i, right, left, far = around("y")
    side = LANES // 2

    @pl.when(c == 0)
    def send_first():
        new = ns_first * low.astype(f32) + jnp.dot(low, p2[...], preferred_element_type=f32)
        ring0[i] = (factor * new).astype(bf16)
        ring = Gather("y", ring0, *lead_halves(LANES), o_send.at[0], o_recv.at[0])
        place = lambda t: out.at[lax.div(t, 2), lax.rem(t, 2)]
        give = lambda t, n: push(ring0.at[t, pl.ds(side, side)], place(t), x_send.at[n], x_recv.at[n], other)
        ring.start()
        over = [give(i, 3)]
        ring.middle()
        ring.nearby()
        over.append(give(left, 4))
        over.append(give(right, 5))
        ring.finish()
        over.append(give(far, 6))
        for t in range(4):
            out[t // 2, t % 2] = ring0[t, 0:side]
        for n, t in enumerate((i, left, right, far)):
            span = pl.ds(pl.multiple_of(lax.rem(t, 2) * HALF, HALF), HALF)
            expected = out.at[lax.div(t, 2), 2, :, span]
            pltpu.make_async_remote_copy(
                src_ref=expected, dst_ref=expected, send_sem=x_send.at[3 + n], recv_sem=x_recv.at[3 + n],
                device_id=other, device_id_type=MESH,
            ).wait_recv()
        for copy in over:
            copy.wait_send()
        ring.drain()

    @pl.when(c == 1)
    def send_second():
        half = pl.ds(pl.multiple_of(h * HALF, HALF), HALF)
        kept = jnp.where(h == 0, first_x[:, 0:HALF], first_x[:, HALF:])
        new = ns_first * kept.astype(bf16).astype(f32) + jnp.dot(
            low, p2[:, half], preferred_element_type=f32
        )
        ring1[i] = (factor * new).astype(bf16)
        ring = Gather("y", ring1, *lead_halves(LANES), o_send.at[1], o_recv.at[1])
        place = lambda t: out.at[lax.div(t, 2), 2, :, pl.ds(pl.multiple_of(lax.rem(t, 2) * HALF, HALF), HALF)]
        give = lambda t, n: push(ring1.at[t, pl.ds(0, side)], place(t), x_send.at[n], x_recv.at[n], other)
        ring.start()
        over = [give(i, 3)]
        ring.middle()
        ring.nearby()
        over.append(give(left, 4))
        over.append(give(right, 5))
        ring.finish()
        over.append(give(far, 6))
        for t in range(4):
            out[t // 2, 2, :, (t % 2) * HALF:(t % 2 + 1) * HALF] = ring1[t, side:]
        for n, t in enumerate((i, left, right, far)):
            expected = out.at[lax.div(t, 2), lax.rem(t, 2)]
            pltpu.make_async_remote_copy(
                src_ref=expected, dst_ref=expected, send_sem=x_send.at[3 + n], recv_sem=x_recv.at[3 + n],
                device_id=other, device_id_type=MESH,
            ).wait_recv()
        for copy in over:
            copy.wait_send()
        ring.drain()

    for copy in swaps:
        copy.wait_send()
    for one in rs0 + ag0 + ag1:
        one.drain()


def per_device(
    token_inputs, cotangent, gate_preact, up_preact, down_weight, block_expert, block_count
):
    done = grad_update(
        block_expert, block_count, cotangent, token_inputs, gate_preact, up_preact,
        down_weight.swapaxes(1, 2),
    )
    return done.swapaxes(2, 3)


def solution(mesh):
    torus = Mesh(mesh.devices.reshape(4, 4, 2, mesh.shape["rep"]), ("z", "x", "core", "y"))
    dp, dp_rep = ("z", "x", "core"), ("z", "x", "core", "y")
    return jax.shard_map(
        per_device,
        mesh=torus,
        in_specs=(
            P(dp_rep, None),
            P(dp_rep, None),
            P(dp_rep, None),
            P(dp_rep, None),
            P(None, None, dp),
            P(dp_rep),
            P(dp_rep),
        ),
        out_specs=P(None, None, None, dp),
        check_vma=False,
    )
```
